512 devices in a mesh: row: 16 (over x, y_hi), col: 32 (over z, y_lo, core).
Axes of the slice: x: 4, y: 8 (y_hi: 4, y_lo: 2; y = y_hi * 2 + y_lo), z: 8, core: 2. Of those that a mesh axis runs over, the one named last changes fastest.
Arguments:
- centers: float32 [3, 65536], P(None, 'row'), may hold values from -896 to 1920, as said below
- normals: float32 [3, 65536], P(None, 'row'), may hold values from -1 to 1, as said below
- areas: float32 [65536], P('row'), may hold values from 3 to 63
- onset: float32 [3, 32], replicated, may hold values from -1 to 1, as said below
- start: float32 [32, 65536], P(None, ('row', 'col')), may hold values from -3 to 3
Outputs:
- strengths: float32 [32, 65536], P(None, ('row', 'col'))
- pressure: float32 [32, 65536], P(None, ('row', 'col'))
The draws below stay inside these ranges and needn't reach their ends.
Inputs may be any that keep to these rules, and one draw needn't show every extreme that they name: `centers`: coordinates of panel collocation points; the panels of a patch form a closed band, ordered as in the reference program. `normals`: each column has unit length. `onset`: each column has unit length.
All inputs are finite; a program needn't handle non-finite values.
Results may differ from the reference program's by a relative error of at most 0.0003.
Values may be sent and summed in bfloat16 or wider, within the bound.
No kernel may reach another device: no remote copies, remote signals or barrier semaphores. Data moves between devices by JAX's collectives and lax.ppermute only.
A program may use at most 64 MiB of HBM per device.

```python
import math
import jax
import jax.numpy as jnp
from jax import lax

N = 65536
K = 32
PA = 64
PB = 32
SWEEPS = 2


def formation(key):
    count = N // (PA * PB)
    keys = jax.random.split(jax.random.fold_in(key, 11), 6)
    index = jnp.arange(count)
    frac = index.astype(jnp.float32) / max(count - 1, 1)
    size = 1.0 + frac
    largest = 2.0
    stretch = 5.0
    unit_radius = PB / (2.0 * math.pi)
    radius = unit_radius * jnp.sqrt(size)
    step = stretch * size * jnp.sqrt(size)
    spacing = 2.35 * unit_radius * math.sqrt(largest)
    across = 2 ** (count.bit_length() // 2)
    column = (index % across).astype(jnp.float32)
    layer = (index // across).astype(jnp.float32)
    shift = jax.random.uniform(keys[0], (3, count), jnp.float32, -1.0, 1.0)
    base_x = spacing * (column + 0.04 * shift[0])
    base_y = spacing * (layer + 0.04 * shift[1])
    base_z = 0.1 * PA * shift[2]
    phase = jax.random.uniform(keys[1], (count,), jnp.float32, 0.0, 2.0 * math.pi)
    jitter_a = jax.random.uniform(keys[2], (count, PA, PB), jnp.float32, -1.0, 1.0)
    jitter_b = jax.random.uniform(keys[3], (count, PA, PB), jnp.float32, -1.0, 1.0)
    line = jnp.arange(PA).astype(jnp.float32)[None, :, None]
    beside_all = jnp.arange(PB).astype(jnp.float32)[None, None, :]
    along = (line - 0.5 * (PA - 1) + 0.15 * jitter_a) * step[:, None, None]
    theta = 2.0 * math.pi * (beside_all + 0.2 * jitter_b) / PB + phase[:, None, None]
    cos_t = jnp.cos(theta)
    sin_t = jnp.sin(theta)
    pos = jnp.stack([base_x[:, None, None] + radius[:, None, None] * cos_t, base_y[:, None, None] + radius[:, None, None] * sin_t, base_z[:, None, None] + along])
    cycle = jnp.stack([cos_t, sin_t, jnp.zeros_like(cos_t)])
    rough = 0.15 * jnp.clip(jax.random.normal(keys[4], (3, count, PA, PB), jnp.float32), -2.0, 2.0)
    tilt = cycle + rough
    normal = tilt / jnp.sqrt(jnp.sum(tilt * tilt, axis=0))
    area = stretch * (size * size)[:, None, None] * jax.random.uniform(keys[5], (count, PA, PB), jnp.float32, 0.6, 1.4)
    return (pos.reshape(3, N), normal.reshape(3, N), area.reshape(N))


def draw_centers(key, part):
    return formation(key)[0]


def draw_normals(key, part):
    return formation(key)[1]


def draw_areas(key, part):
    return formation(key)[2]


def draw_onset(key, part):
    keys = jax.random.split(jax.random.fold_in(key, 23), 2)
    azimuth = jax.random.uniform(keys[0], (K,), jnp.float32, -math.pi, math.pi)
    elevation = jax.random.uniform(keys[1], (K,), jnp.float32, -0.6, 0.6)
    return jnp.stack([jnp.cos(elevation) * jnp.cos(azimuth), jnp.cos(elevation) * jnp.sin(azimuth), jnp.sin(elevation)])


def levels(key, shape, pieces, least, high):
    def one(axis_at, shards_of):
        heights = jax.random.uniform(jax.random.fold_in(jax.random.fold_in(key, 6), axis_at), (shards_of,), jnp.float32, least / len(pieces), high / len(pieces))
        return jnp.repeat(jnp.exp(heights), shape[axis_at] // shards_of).reshape((-1,) + (1,) * (len(shape) - axis_at - 1))

    loudness = one(*pieces[0])
    for cut in pieces[1:]:
        loudness = loudness * one(*cut)
    return loudness


def scatter_about(key, extent, deviation, most, pieces=(), dtype=jnp.bfloat16):
    loudness = levels(key, extent, pieces, -0.22, 0.18) if pieces else 1.0
    entries = jax.random.normal(key, extent, jnp.float32) * deviation * loudness
    return jnp.minimum(jnp.maximum(entries, -most), most).astype(dtype)


def setup_inputs(seed: int = 0) -> dict:
    key_of = jax.random.split(jax.random.key(seed), 6)
    centers = draw_centers(jax.random.fold_in(key_of[5], 71), 0)
    normals = draw_normals(jax.random.fold_in(key_of[5], 71), 0)
    areas = draw_areas(jax.random.fold_in(key_of[5], 71), 0)
    onset = draw_onset(jax.random.fold_in(key_of[5], 71), 0)
    start = scatter_about(key_of[4], (K, N), 0.5, 3.0, ((1, 512),), jnp.float32)
    return dict(centers=centers, normals=normals, areas=areas, onset=onset, start=start)


INV_FOUR_PI = 1.0 / (4.0 * math.pi)
CAP = 0.4
OMEGA = 1.5
EPS = 1e-06

def kernel_block(src_centers, src_normals, src_areas, dst_centers):
    delta_x = dst_centers[0][None, :] - src_centers[0][:, None]
    delta_y = dst_centers[1][None, :] - src_centers[1][:, None]
    delta_z = dst_centers[2][None, :] - src_centers[2][:, None]
    dist_sq = delta_x * delta_x + delta_y * delta_y + delta_z * delta_z + src_areas[:, None]
    inverse = lax.rsqrt(dist_sq)
    facing = src_normals[0][:, None] * delta_x + src_normals[1][:, None] * delta_y + src_normals[2][:, None] * delta_z
    value = (src_areas * INV_FOUR_PI)[:, None] * facing * (inverse * inverse * inverse)
    return value.astype(jnp.bfloat16)

def surface_pressure(strengths, centers, onset):
    fields = jnp.concatenate([strengths, centers], axis=0).reshape(K + 3, N // PB, PB)
    upper = jnp.concatenate([fields[:, 1:], fields[:, -1:]], axis=1)
    lower = jnp.concatenate([fields[:, :1], fields[:, :-1]], axis=1)
    after = jnp.roll(fields, -1, axis=2)
    before = jnp.roll(fields, 1, axis=2)
    diff_a = upper - lower
    diff_b = after - before
    span_a = jnp.sqrt(lax.optimization_barrier(jnp.sum(diff_a[K:] * diff_a[K:], axis=0)))
    span_b = jnp.sqrt(lax.optimization_barrier(jnp.sum(diff_b[K:] * diff_b[K:], axis=0)))
    onset_a = lax.optimization_barrier(jnp.sum(onset[:, :, None, None] * diff_a[K:][:, None], axis=0)) / span_a
    onset_b = lax.optimization_barrier(jnp.sum(onset[:, :, None, None] * diff_b[K:][:, None], axis=0)) / span_b
    speed_a = onset_a - diff_a[:K] / span_a
    speed_b = onset_b - diff_b[:K] / span_b
    pressure = 1.0 - speed_a * speed_a - speed_b * speed_b
    return pressure.reshape(K, N)

def reference(centers, normals, areas, onset, start):
    right = -lax.optimization_barrier(jnp.sum(onset[:, :, None] * normals[:, None, :], axis=0))
    total = jnp.sum(areas)
    strengths = start
    for sweep in range(SWEEPS):
        moved = strengths.astype(jnp.bfloat16)

        def add_block(index, acc):
            first = (index * 256).astype(jnp.int32)
            src_c = lax.dynamic_slice_in_dim(centers, first, 256, 1)
            src_n = lax.dynamic_slice_in_dim(normals, first, 256, 1)
            src_a = lax.dynamic_slice_in_dim(areas, first, 256, 0)
            tile = kernel_block(src_c, src_n, src_a, centers)
            part = lax.dynamic_slice_in_dim(moved, first, 256, 1)
            return acc + jnp.dot(part, tile, preferred_element_type=jnp.float32)
        product = lax.fori_loop(jnp.int32(0), jnp.int32(N // 256), add_block, jnp.zeros((K, N), jnp.float32))
        residual = right - 0.5 * strengths - product
        sums = lax.optimization_barrier(jnp.sum(areas[None, :] * residual * residual, axis=1))
        scale = jnp.minimum(1.0, CAP * jnp.sqrt(total) * lax.rsqrt(sums + EPS))
        strengths = strengths + OMEGA * scale[:, None] * residual
    pressure = surface_pressure(strengths, centers, onset)
    return (strengths, pressure)
```

```python
import math

import jax
import jax.numpy as jnp
from jax import lax
from jax.experimental import pallas as pl
from jax.experimental.pallas import tpu as pltpu
from jax.sharding import PartitionSpec as P

PB = 32
SWEEPS = 2


INV_FOUR_PI = 1.0 / (4.0 * math.pi)
CAP = 0.4
OMEGA = 1.5
EPS = 1e-06
LANES = 128
STEP = 256


def spread(block, axis, count):
    copies = jnp.broadcast_to(block[None], (count,) + block.shape)
    return lax.all_to_all(copies, axis, 0, 0, tiled=True)


def build_kernel(source_ref, target_ref, moved_ref, tile_ref, product_ref, wide_ref):
    step = pl.program_id(0)
    targets = target_ref.shape[1]

    for row in range(7):
        column = source_ref[:, row : row + 1]
        wide_ref[row] = jnp.broadcast_to(column, (STEP, LANES))

    def rows(index, carry):
        at = pl.ds(pl.multiple_of(index * 16, 16), 16)
        src_x, src_y, src_z = wide_ref[0, at, :], wide_ref[1, at, :], wide_ref[2, at, :]
        nor_x, nor_y, nor_z = wide_ref[3, at, :], wide_ref[4, at, :], wide_ref[5, at, :]
        area = wide_ref[6, at, :]
        for lane in range(0, targets, LANES):
            here = slice(lane, lane + LANES)
            delta_x = target_ref[0:1, here] - src_x
            delta_y = target_ref[1:2, here] - src_y
            delta_z = target_ref[2:3, here] - src_z
            dist_sq = delta_x * delta_x + delta_y * delta_y + delta_z * delta_z + area
            inverse = lax.rsqrt(dist_sq)
            facing = nor_x * delta_x + nor_y * delta_y + nor_z * delta_z
            value = facing * (inverse * inverse * inverse)
            tile_ref[at, here] = value.astype(jnp.bfloat16)
        return carry

    lax.fori_loop(0, STEP // 16, rows, 0)

    part = jnp.concatenate([moved_ref[i] for i in range(STEP // LANES)], axis=1)
    product = jnp.dot(part, tile_ref[...], preferred_element_type=jnp.float32)

    @pl.when(step == 0)
    def _():
        for chunk in range(targets // LANES):
            product_ref[chunk] = product[:, chunk * LANES : (chunk + 1) * LANES]

    @pl.when(step > 0)
    def _():
        for chunk in range(targets // LANES):
            product_ref[chunk] += product[:, chunk * LANES : (chunk + 1) * LANES]


def build(sources, targets, moved):
    count = sources.shape[0]
    width = targets.shape[1]
    blocks, onsets, _ = moved.shape
    return pl.pallas_call(
        build_kernel,
        grid=(count // STEP,),
        in_specs=[
            pl.BlockSpec((STEP, 8), lambda i: (i, 0)),
            pl.BlockSpec((8, width), lambda i: (0, 0)),
            pl.BlockSpec((STEP // LANES, onsets, LANES), lambda i: (i, 0, 0)),
        ],
        out_specs=[
            pl.BlockSpec((STEP, width), lambda i: (i, 0)),
            pl.BlockSpec((width // LANES, onsets, LANES), lambda i: (0, 0, 0)),
        ],
        out_shape=[
            jax.ShapeDtypeStruct((count, width), jnp.bfloat16),
            jax.ShapeDtypeStruct((width // LANES, onsets, LANES), jnp.float32),
        ],
        scratch_shapes=[pltpu.VMEM((7, STEP, LANES), jnp.float32)],
        compiler_params=pltpu.CompilerParams(vmem_limit_bytes=40 << 20),
        name="build",
    )(sources, targets, moved)


def apply_kernel(moved_ref, tile_ref, product_ref):
    step = pl.program_id(0)
    targets = tile_ref.shape[1]
    blocks = tile_ref.shape[0] // LANES
    part = jnp.concatenate([moved_ref[i] for i in range(blocks)], axis=1)
    product = jnp.dot(part, tile_ref[...], preferred_element_type=jnp.float32)

    @pl.when(step == 0)
    def _():
        for chunk in range(targets // LANES):
            product_ref[chunk] = product[:, chunk * LANES : (chunk + 1) * LANES]

    @pl.when(step > 0)
    def _():
        for chunk in range(targets // LANES):
            product_ref[chunk] += product[:, chunk * LANES : (chunk + 1) * LANES]


def apply(tile, moved, depth=512):
    count, width = tile.shape
    blocks, onsets, _ = moved.shape
    return pl.pallas_call(
        apply_kernel,
        grid=(count // depth,),
        in_specs=[
            pl.BlockSpec((depth // LANES, onsets, LANES), lambda i: (i, 0, 0)),
            pl.BlockSpec((depth, width), lambda i: (i, 0)),
        ],
        out_specs=pl.BlockSpec((width // LANES, onsets, LANES), lambda i: (0, 0, 0)),
        out_shape=jax.ShapeDtypeStruct((width // LANES, onsets, LANES), jnp.float32),
        compiler_params=pltpu.CompilerParams(vmem_limit_bytes=40 << 20),
        name="apply",
    )(moved, tile)


def in_three(value):
    high = lax.reduce_precision(value, 8, 7)
    rest = value - high
    middle = lax.reduce_precision(rest, 8, 7)
    return high, middle, rest - middle


def per_device(centers, normals, areas, onset, start):
    row_count = lax.axis_size("row")
    col_count = lax.axis_size("col")
    row_index = lax.axis_index("row")
    col_index = lax.axis_index("col")
    own = start.shape[1]
    count = start.shape[0]
    own_first = col_index * own
    own_areas = lax.dynamic_slice_in_dim(areas, own_first, own, 0)
    own_normals = lax.dynamic_slice_in_dim(normals, own_first, own, 1)
    own_centers = lax.dynamic_slice_in_dim(centers, own_first, own, 1)

    block_area = jnp.broadcast_to(jnp.sum(areas), (1, own))
    note = jnp.concatenate([own_centers, block_area, jnp.zeros((4, own), jnp.float32)], axis=0)
    notes = spread(note, "row", row_count)
    targets = jnp.transpose(notes, (1, 0, 2)).reshape(8, row_count * own)
    total = jnp.sum(notes[:, 3, 0])
    moved = spread(start.astype(jnp.bfloat16), "col", col_count)

    sources = jnp.concatenate(
        [centers, normals * (areas * INV_FOUR_PI)[None, :], areas[None, :], areas[None, :]], axis=0
    ).T
    tile, partial = build(sources, targets, moved)

    product = jnp.sum(lax.all_to_all(partial, "row", 0, 0, tiled=True), axis=0)
    right = -jnp.sum(onset[:, :, None] * own_normals[:, None, :], axis=0)
    residual = right - 0.5 * start - product
    part = jnp.sum(own_areas[None, :] * residual * residual, axis=1)
    high, middle, low = in_three(part)
    line = jnp.concatenate([high, middle, low, jnp.zeros_like(low)])[None, :]
    line = jnp.concatenate([line, jnp.zeros((15, own), jnp.float32)], axis=0)
    sent = jnp.concatenate([residual, line], axis=0).astype(jnp.bfloat16)
    gathered = spread(sent, "col", col_count)
    parts = jnp.sum(gathered[:, count, :].astype(jnp.float32), axis=0)
    block_sum = parts[:count] + (parts[count : 2 * count] + parts[2 * count : 3 * count])
    partial = apply(tile, gathered[:, :count, :])
    extra = jnp.broadcast_to(jnp.pad(block_sum, (0, own - count))[None, None], (row_count, 8, own))
    swapped = jnp.sum(
        lax.all_to_all(jnp.concatenate([partial, extra], axis=1), "row", 0, 0, tiled=True), axis=0
    )
    change = swapped[:count]
    sums = swapped[count, :count]
    weight = OMEGA * jnp.minimum(1.0, CAP * jnp.sqrt(total) * lax.rsqrt(sums + EPS))[:, None]
    state = start + weight * residual
    product = product + weight * change
    residual = right - 0.5 * state - product

    flat = row_index * col_count + col_index
    devices = row_count * col_count
    edges = jnp.concatenate([state, residual, own_centers], axis=0)
    forward = [(i, i + 1) for i in range(devices - 1)]
    backward = [(i + 1, i) for i in range(devices - 1)]
    before = lax.ppermute(edges[:, own - PB :], ("row", "col"), forward)
    after = lax.ppermute(edges[:, :PB], ("row", "col"), backward)

    part = jnp.sum(own_areas[None, :] * residual * residual, axis=1)
    part = jnp.broadcast_to(jnp.pad(part, (0, own - count))[None], (8, own))
    part = jnp.sum(spread(part, "col", col_count), axis=0)
    sums = jnp.sum(spread(part, "row", row_count), axis=0)[0, :count]
    weight = OMEGA * jnp.minimum(1.0, CAP * jnp.sqrt(total) * lax.rsqrt(sums + EPS))[:, None]

    def finish(edge):
        return jnp.concatenate(
            [edge[:count] + weight * edge[count : 2 * count], edge[2 * count :]], axis=0
        )

    fields = finish(edges)
    state = fields[:count]
    before = jnp.where(flat == 0, fields[:, :PB], finish(before))
    after = jnp.where(flat == devices - 1, fields[:, own - PB :], finish(after))
    padded = jnp.concatenate([before, fields, after], axis=1)
    diff_a = padded[:, 2 * PB :] - padded[:, : own]
    lane = lax.broadcasted_iota(jnp.int32, fields.shape, 1) % PB
    following = jnp.where(lane == PB - 1, jnp.roll(fields, PB - 1, 1), jnp.roll(fields, -1, 1))
    preceding = jnp.where(lane == 0, jnp.roll(fields, 1 - PB, 1), jnp.roll(fields, 1, 1))
    diff_b = following - preceding
    speeds = []
    for diff in (diff_a, diff_b):
        step = diff[count:]
        span = jnp.sqrt(jnp.sum(step * step, axis=0))
        along = jnp.sum(onset[:, :, None] * step[:, None, :], axis=0)
        speeds.append(along / span - diff[:count] / span)
    pressure = 1.0 - speeds[0] * speeds[0] - speeds[1] * speeds[1]
    return (state, pressure)


def solution(mesh):
    return jax.shard_map(
        per_device,
        mesh=mesh,
        in_specs=(P(None, "row"), P(None, "row"), P("row"), P(), P(None, ("row", "col"))),
        out_specs=(P(None, ("row", "col")), P(None, ("row", "col"))),
        check_vma=False,
    )
```

```python
import math

import jax
import jax.numpy as jnp
from jax import lax
from jax.experimental import pallas as pl
from jax.experimental.pallas import tpu as pltpu
from jax.sharding import PartitionSpec as P

PB = 32
SWEEPS = 2


INV_FOUR_PI = 1.0 / (4.0 * math.pi)
CAP = 0.4
OMEGA = 1.5
EPS = 1e-06
LANES = 128
STEP = 256
BLOCK = 512
VMEM_BYTES = 58 << 20


def spread(block, axis, count):
    copies = jnp.broadcast_to(block[None], (count,) + block.shape)
    return lax.all_to_all(copies, axis, 0, 0, tiled=True)


def fill(source_ref, wide_ref, tile_refs, first):
    targets = wide_ref.shape[2]
    for half in range(0, 32, 16):
        at = pl.ds(pl.multiple_of(first + half, 16), 16)
        params = [
            jnp.broadcast_to(source_ref[at, row : row + 1], (16, LANES)) for row in range(7)
        ]
        src_x, src_y, src_z, nor_x, nor_y, nor_z, area = params
        for lane in range(0, targets, LANES):
            here = slice(lane, lane + LANES)
            delta_x = wide_ref[0, :, here] - src_x
            delta_y = wide_ref[1, :, here] - src_y
            delta_z = wide_ref[2, :, here] - src_z
            dist_sq = delta_x * delta_x + delta_y * delta_y + delta_z * delta_z + area
            inverse = lax.rsqrt(dist_sq)
            facing = nor_x * delta_x + nor_y * delta_y + nor_z * delta_z
            value = (facing * (inverse * inverse * inverse)).astype(jnp.bfloat16)
            for tile_ref in tile_refs:
                tile_ref[at, here] = value


def widen(target_ref, wide_ref):
    for row in range(3):
        wide_ref[row] = jnp.broadcast_to(target_ref[row : row + 1, :], wide_ref.shape[1:])


def build_kernel(source_ref, target_ref, tile_ref, wide_ref):
    @pl.when(pl.program_id(0) == 0)
    def _():
        widen(target_ref, wide_ref)

    def rows(index, carry):
        fill(source_ref, wide_ref, [tile_ref], index * 32)
        return carry

    lax.fori_loop(0, BLOCK // 32, rows, 0)


def finish_kernel(
    source_ref, target_ref, moved_ref, old_ref, tile_ref, product_ref, wide_ref, kept_ref
):
    step = pl.program_id(0)
    blocks = pl.num_programs(0) - 1
    columns = tile_ref.shape[1] // STEP
    now = step % 2
    before = 1 - now

    @pl.when(step == 0)
    def _():
        widen(target_ref, wide_ref)
        product_ref[...] = jnp.zeros_like(product_ref)

    def part_of(block):
        return jnp.concatenate([moved_ref[2 * block], moved_ref[2 * block + 1]], axis=1)

    def dot(block, value):
        return jnp.dot(part_of(block), value, preferred_element_type=jnp.float32)

    def place(index):
        down, column = index // columns, index % columns
        rows = pl.ds(pl.multiple_of(down * STEP, STEP), STEP)
        lanes = pl.ds(pl.multiple_of(column * STEP, STEP), STEP)
        return down, column, rows, lanes

    def add_to(column, value):
        product_ref[2 * column] += value[:, :LANES]
        product_ref[2 * column + 1] += value[:, LANES:]

    deep = BLOCK // STEP
    offset = blocks * deep

    @pl.when(step == 0)
    def _():
        def each(index, carry):
            down, column, rows, lanes = place(index)
            fill(source_ref, wide_ref, [tile_ref, kept_ref.at[now]], index * 32)
            add_to(column, dot(down, old_ref[rows, lanes]))
            return carry

        lax.fori_loop(0, BLOCK // 32, each, 0)

    @pl.when((step > 0) & (step < blocks))
    def _():
        def each(index, carry):
            down, column, rows, lanes = place(index)
            fill(source_ref, wide_ref, [tile_ref, kept_ref.at[now]], index * 32)
            value = dot(step * deep + down, old_ref[rows, lanes])
            value += dot(offset + (step - 1) * deep + down, kept_ref[before, rows, lanes])
            add_to(column, value)
            return carry

        lax.fori_loop(0, BLOCK // 32, each, 0)

    @pl.when(step == blocks)
    def _():
        def each(index, carry):
            down, column, rows, lanes = place(index)
            add_to(column, dot(offset + (step - 1) * deep + down, kept_ref[before, rows, lanes]))
            return carry

        lax.fori_loop(0, deep * columns, each, 0)


def build(sources, targets, count):
    width = targets.shape[1]
    return pl.pallas_call(
        build_kernel,
        grid=(count // BLOCK,),
        in_specs=[
            pl.BlockSpec((BLOCK, 8), lambda i: (i, 0)),
            pl.BlockSpec((8, width), lambda i: (0, 0)),
        ],
        out_specs=pl.BlockSpec((BLOCK, width), lambda i: (i, 0)),
        out_shape=pltpu.HBM((count, width), jnp.bfloat16),
        scratch_shapes=[pltpu.VMEM((3, 16, width), jnp.float32)],
        compiler_params=pltpu.CompilerParams(vmem_limit_bytes=VMEM_BYTES),
        cost_estimate=pl.CostEstimate(
            flops=count * width * 18, bytes_accessed=count * width * 2, transcendentals=count * width
        ),
        name="build",
    )(sources, targets)


def finish_build(sources, targets, moved, old):
    count, width = old.shape
    blocks = count // BLOCK
    onsets = moved.shape[1]
    return pl.pallas_call(
        finish_kernel,
        grid=(blocks + 1,),
        in_specs=[
            pl.BlockSpec((BLOCK, 8), lambda i: (blocks + jnp.minimum(i, blocks - 1), 0)),
            pl.BlockSpec((8, width), lambda i: (0, 0)),
            pl.BlockSpec(moved.shape, lambda i: (0, 0, 0)),
            pl.BlockSpec((BLOCK, width), lambda i: (jnp.minimum(i, blocks - 1), 0)),
        ],
        out_specs=[
            pl.BlockSpec((BLOCK, width), lambda i: (jnp.minimum(i, blocks - 1), 0)),
            pl.BlockSpec((width // LANES, onsets, LANES), lambda i: (0, 0, 0)),
        ],
        out_shape=[
            pltpu.HBM((count, width), jnp.bfloat16),
            jax.ShapeDtypeStruct((width // LANES, onsets, LANES), jnp.float32),
        ],
        scratch_shapes=[
            pltpu.VMEM((3, 16, width), jnp.float32),
            pltpu.VMEM((2, BLOCK, width), jnp.bfloat16),
        ],
        compiler_params=pltpu.CompilerParams(vmem_limit_bytes=VMEM_BYTES),
        name="finish",
    )(sources, targets, moved, old)


def apply_kernel(early_ref, late_ref, old_ref, tile_ref, product_ref):
    step = pl.program_id(0)

    def wide(ref):
        return jnp.concatenate([ref[i] for i in range(ref.shape[0])], axis=1)

    early, late = wide(early_ref), wide(late_ref)
    for column in range(tile_ref.shape[1] // STEP):
        lanes = slice(column * STEP, (column + 1) * STEP)
        value = jnp.dot(early, old_ref[:, lanes], preferred_element_type=jnp.float32)
        value += jnp.dot(late, tile_ref[:, lanes], preferred_element_type=jnp.float32)

        @pl.when(step == 0)
        def _():
            product_ref[2 * column] = value[:, :LANES]
            product_ref[2 * column + 1] = value[:, LANES:]

        @pl.when(step > 0)
        def _():
            product_ref[2 * column] += value[:, :LANES]
            product_ref[2 * column + 1] += value[:, LANES:]


def apply(moved, old, tile, depth=256):
    count, width = tile.shape
    onsets = moved.shape[1]
    steps = count // depth
    return pl.pallas_call(
        apply_kernel,
        grid=(steps,),
        in_specs=[
            pl.BlockSpec((depth // LANES, onsets, LANES), lambda i: (i, 0, 0)),
            pl.BlockSpec((depth // LANES, onsets, LANES), lambda i: (steps + i, 0, 0)),
            pl.BlockSpec((depth, width), lambda i: (i, 0)),
            pl.BlockSpec((depth, width), lambda i: (i, 0)),
        ],
        out_specs=pl.BlockSpec((width // LANES, onsets, LANES), lambda i: (0, 0, 0)),
        out_shape=jax.ShapeDtypeStruct((width // LANES, onsets, LANES), jnp.float32),
        compiler_params=pltpu.CompilerParams(vmem_limit_bytes=VMEM_BYTES),
        name="apply",
    )(moved, moved, old, tile)


def per_device(centers, normals, areas, onset, start):
    row_count = lax.axis_size("row")
    col_count = lax.axis_size("col")
    row_index = lax.axis_index("row")
    col_index = lax.axis_index("col")
    own = start.shape[1]
    count = start.shape[0]
    own_first = col_index * own
    own_areas = lax.dynamic_slice_in_dim(areas, own_first, own, 0)
    own_normals = lax.dynamic_slice_in_dim(normals, own_first, own, 1)
    own_centers = lax.dynamic_slice_in_dim(centers, own_first, own, 1)

    note = jnp.concatenate([own_centers, jnp.zeros((5, own), jnp.float32)], axis=0)
    notes = spread(note, "row", row_count)
    targets = jnp.transpose(notes, (1, 0, 2)).reshape(8, row_count * own)
    shown = lax.optimization_barrier((start, notes))[0]
    moved = spread(shown.astype(jnp.bfloat16), "col", col_count)

    sources = jnp.concatenate(
        [centers, normals * (areas * INV_FOUR_PI)[None, :], areas[None, :], areas[None, :]], axis=0
    ).T
    old = build(sources, targets, sources.shape[0] // 2)
    tile, partial = finish_build(sources, targets, moved, old)

    product = jnp.sum(lax.all_to_all(partial, "row", 0, 0, tiled=True), axis=0)
    right = -jnp.sum(onset[:, :, None] * own_normals[:, None, :], axis=0)
    residual = right - 0.5 * start - product
    gathered = spread(residual.astype(jnp.bfloat16), "col", col_count)
    partial = apply(gathered, old, tile)
    change = jnp.sum(lax.all_to_all(partial, "row", 0, 0, tiled=True), axis=0)

    flat = row_index * col_count + col_index
    devices = row_count * col_count
    edges = jnp.concatenate([start, residual, change, own_centers], axis=0)
    forward = [(i, i + 1) for i in range(devices - 1)]
    backward = [(i + 1, i) for i in range(devices - 1)]
    before = lax.ppermute(edges[:, own - PB :], ("row", "col"), forward)
    after = lax.ppermute(edges[:, :PB], ("row", "col"), backward)

    weighted = own_areas[None, :] * residual
    part = jnp.concatenate(
        [
            jnp.sum(weighted * residual, axis=1),
            jnp.sum(weighted * change, axis=1),
            jnp.sum(own_areas[None, :] * change * change, axis=1),
            jnp.broadcast_to(jnp.sum(own_areas), (count,)),
        ]
    )
    part = jnp.broadcast_to(part[None], (8, 4 * count))
    part = jnp.sum(spread(part, "col", col_count), axis=0)
    part = jnp.sum(spread(part, "row", row_count), axis=0)[0]
    both = part[:count]
    mixed = part[count : 2 * count]
    changed = part[2 * count : 3 * count]
    reach = CAP * jnp.sqrt(part[3 * count])

    def damp(sums):
        return OMEGA * jnp.minimum(1.0, reach * lax.rsqrt(sums + EPS))

    one = damp(both)
    keep = 1.0 - 0.5 * one
    sums = keep * keep * both - 2.0 * keep * one * mixed + one * one * changed
    two = damp(jnp.maximum(sums, 0.0))
    on_residual = (one + two * keep)[:, None]
    on_change = (two * one)[:, None]

    def finish(edge):
        strengths = edge[:count] + on_residual * edge[count : 2 * count]
        strengths = strengths - on_change * edge[2 * count : 3 * count]
        return jnp.concatenate([strengths, edge[3 * count :]], axis=0)

    fields = finish(edges)
    state = fields[:count]
    before = jnp.where(flat == 0, fields[:, :PB], finish(before))
    after = jnp.where(flat == devices - 1, fields[:, own - PB :], finish(after))
    padded = jnp.concatenate([before, fields, after], axis=1)
    diff_a = padded[:, 2 * PB :] - padded[:, :own]
    lane = lax.broadcasted_iota(jnp.int32, fields.shape, 1) % PB
    following = jnp.where(lane == PB - 1, jnp.roll(fields, PB - 1, 1), jnp.roll(fields, -1, 1))
    preceding = jnp.where(lane == 0, jnp.roll(fields, 1 - PB, 1), jnp.roll(fields, 1, 1))
    diff_b = following - preceding
    speeds = []
    for diff in (diff_a, diff_b):
        step = diff[count:]
        span = jnp.sqrt(jnp.sum(step * step, axis=0))
        along = jnp.sum(onset[:, :, None] * step[:, None, :], axis=0)
        speeds.append(along / span - diff[:count] / span)
    pressure = 1.0 - speeds[0] * speeds[0] - speeds[1] * speeds[1]
    return (state, pressure)


def solution(mesh):
    return jax.shard_map(
        per_device,
        mesh=mesh,
        in_specs=(P(None, "row"), P(None, "row"), P("row"), P(), P(None, ("row", "col"))),
        out_specs=(P(None, ("row", "col")), P(None, ("row", "col"))),
        check_vma=False,
    )
```

```python
import math

import jax
import jax.numpy as jnp
from jax import lax
from jax.experimental import pallas as pl
from jax.experimental.pallas import tpu as pltpu
from jax.sharding import PartitionSpec as P

PB = 32
SWEEPS = 2


INV_FOUR_PI = 1.0 / (4.0 * math.pi)
CAP = 0.4
OMEGA = 1.5
EPS = 1e-06
LANES = 128
STEP = 256
BLOCK = 512
VMEM_BYTES = 58 << 20


def spread(block, axis, count):
    copies = jnp.broadcast_to(block[None], (count,) + block.shape)
    return lax.all_to_all(copies, axis, 0, 0, tiled=True)


def three(value):
    high = value.astype(jnp.bfloat16).astype(jnp.float32)
    rest = value - high
    middle = rest.astype(jnp.bfloat16).astype(jnp.float32)
    return high, middle, rest - middle


def factor_kernel(place_ref, normal_ref, factor_ref):
    place = place_ref[...]
    scaled = normal_ref[...] * (place[3:4, :] * INV_FOUR_PI)
    level = -jnp.sum(scaled * place, axis=0, keepdims=True)
    at_level = lax.broadcasted_iota(jnp.int32, place.shape, 0) == 3
    high, middle, low = three(jnp.where(at_level, level, scaled))
    bare = jnp.where(at_level, 0.0, high)
    bare_middle = jnp.where(at_level, 0.0, middle)
    none = jnp.zeros_like(high)
    rows = [high, bare, middle, bare, bare_middle, low, none, none]
    rows += list(three(place)) + [none] * 5
    factor_ref[...] = jnp.concatenate(rows, axis=0).T.astype(jnp.bfloat16)


def source_factors(place, normal):
    count = place.shape[1]
    return pl.pallas_call(
        factor_kernel,
        grid=(count // BLOCK,),
        in_specs=[pl.BlockSpec((8, BLOCK), lambda i: (0, i))] * 2,
        out_specs=pl.BlockSpec((BLOCK, LANES), lambda i: (i, 0)),
        out_shape=jax.ShapeDtypeStruct((count, LANES), jnp.bfloat16),
        cost_estimate=pl.CostEstimate(
            flops=count * 400, bytes_accessed=count * 320, transcendentals=0
        ),
        name="factors",
    )(place, normal)


def target_factors(targets):
    high = targets.astype(jnp.bfloat16).astype(jnp.float32)
    rest = targets - high
    middle = rest.astype(jnp.bfloat16).astype(jnp.float32)
    low = rest - middle
    rows = [high, middle, high, low, middle, high]
    return jnp.concatenate(rows, axis=0).astype(jnp.bfloat16)


def fill(factor_ref, target_ref, wide_ref, pair_ref, column, stores):
    facing = jnp.dot(
        factor_ref[:, :48],
        pair_ref[:, column : column + STEP],
        preferred_element_type=jnp.float32,
    )
    for lane in range(0, STEP, LANES):
        here = slice(column + lane, column + lane + LANES)
        x, y, z = (target_ref[d : d + 1, here] for d in range(3))
        for row in range(0, BLOCK, 16):
            at = slice(row, row + 16)
            delta_x = x - wide_ref[0, at, :]
            delta_y = y - wide_ref[1, at, :]
            delta_z = z - wide_ref[2, at, :]
            dist_sq = delta_x * delta_x + delta_y * delta_y + delta_z * delta_z + wide_ref[3, at, :]
            inverse = lax.rsqrt(dist_sq)
            value = facing[row : row + 16, lane : lane + LANES] * (inverse * inverse * inverse)
            value = value.astype(jnp.bfloat16)
            for store in stores:
                store[at, here] = value


def prepare(target_ref, pair_ref, spread_ref):
    pair_ref[...] = target_factors(target_ref[...])
    which = lax.broadcasted_iota(jnp.int32, spread_ref.shape, 0)
    lane = lax.broadcasted_iota(jnp.int32, spread_ref.shape, 1)
    chosen = which % 8 == lane // LANES
    spread_ref[...] = jnp.where(chosen, 1.0, 0.0).astype(jnp.bfloat16)


def spread_params(factor_ref, spread_ref, wide_ref):
    wide = jnp.dot(factor_ref[:, 64:96], spread_ref[...], preferred_element_type=jnp.float32)
    for row in range(4):
        wide_ref[row] = wide[:, row * LANES : (row + 1) * LANES]


def build_kernel(factor_ref, target_ref, tile_ref, wide_ref, pair_ref, spread_ref):
    @pl.when(pl.program_id(0) == 0)
    def _():
        prepare(target_ref, pair_ref, spread_ref)

    spread_params(factor_ref, spread_ref, wide_ref)
    for column in range(0, tile_ref.shape[1], STEP):
        fill(factor_ref, target_ref, wide_ref, pair_ref, column, [tile_ref])


def finish_kernel(
    factor_ref,
    target_ref,
    moved_ref,
    old_ref,
    tile_ref,
    product_ref,
    wide_ref,
    pair_ref,
    spread_ref,
    even_ref,
    odd_ref,
):
    step = pl.program_id(0)
    blocks = pl.num_programs(0) - 1
    width = tile_ref.shape[1]
    deep = BLOCK // LANES

    @pl.when(step == 0)
    def _():
        prepare(target_ref, pair_ref, spread_ref)
        product_ref[...] = jnp.zeros_like(product_ref)

    def dot(block, ref, column):
        part = jnp.concatenate([moved_ref[deep * block + i] for i in range(deep)], axis=1)
        return jnp.dot(
            part, ref[:, column : column + STEP], preferred_element_type=jnp.float32
        )

    def add_to(column, value):
        for lane in range(0, STEP, LANES):
            product_ref[(column + lane) // LANES] += value[:, lane : lane + LANES]

    def whole(now_ref, before_ref):
        spread_params(factor_ref, spread_ref, wide_ref)
        for column in range(0, width, STEP):
            value = dot(step, old_ref, column)
            if before_ref is not None:
                value += dot(blocks + step - 1, before_ref, column)
            fill(
                factor_ref, target_ref, wide_ref, pair_ref, column, [tile_ref, now_ref]
            )
            add_to(column, value)

    @pl.when(step == 0)
    def _():
        whole(even_ref, None)

    @pl.when((step > 0) & (step < blocks) & (step % 2 == 0))
    def _():
        whole(even_ref, odd_ref)

    @pl.when((step < blocks) & (step % 2 == 1))
    def _():
        whole(odd_ref, even_ref)

    @pl.when((step == blocks) & (step % 2 == 0))
    def _():
        for column in range(0, width, STEP):
            add_to(column, dot(blocks + step - 1, odd_ref, column))

    @pl.when((step == blocks) & (step % 2 == 1))
    def _():
        for column in range(0, width, STEP):
            add_to(column, dot(blocks + step - 1, even_ref, column))


def build(factors, targets):
    count = factors.shape[0]
    width = targets.shape[1]
    return pl.pallas_call(
        build_kernel,
        grid=(count // BLOCK // 2,),
        in_specs=[
            pl.BlockSpec((BLOCK, LANES), lambda i: (i, 0)),
            pl.BlockSpec((8, width), lambda i: (0, 0)),
        ],
        out_specs=pl.BlockSpec((BLOCK, width), lambda i: (i, 0)),
        out_shape=pltpu.HBM((count, width), jnp.bfloat16),
        scratch_shapes=[
            pltpu.VMEM((4, BLOCK, LANES), jnp.float32),
            pltpu.VMEM((48, width), jnp.bfloat16),
            pltpu.VMEM((32, 4 * LANES), jnp.bfloat16),
        ],
        compiler_params=pltpu.CompilerParams(vmem_limit_bytes=VMEM_BYTES),
        cost_estimate=pl.CostEstimate(
            flops=count * width * 50, bytes_accessed=count * width, transcendentals=count * width // 2
        ),
        name="build",
    )(factors, targets)


def finish_build(factors, targets, moved, tile):
    count, width = tile.shape
    blocks = count // BLOCK // 2
    onsets = moved.shape[1]
    return pl.pallas_call(
        finish_kernel,
        grid=(blocks + 1,),
        in_specs=[
            pl.BlockSpec((BLOCK, LANES), lambda i: (blocks + jnp.minimum(i, blocks - 1), 0)),
            pl.BlockSpec((8, width), lambda i: (0, 0)),
            pl.BlockSpec(moved.shape, lambda i: (0, 0, 0)),
            pl.BlockSpec((BLOCK, width), lambda i: (jnp.minimum(i, blocks - 1), 0)),
        ],
        out_specs=[
            pl.BlockSpec((BLOCK, width), lambda i: (blocks + jnp.minimum(i, blocks - 1), 0)),
            pl.BlockSpec((width // LANES, onsets, LANES), lambda i: (0, 0, 0)),
        ],
        out_shape=[
            pltpu.HBM((count, width), jnp.bfloat16),
            jax.ShapeDtypeStruct((width // LANES, onsets, LANES), jnp.float32),
        ],
        scratch_shapes=[
            pltpu.VMEM((4, BLOCK, LANES), jnp.float32),
            pltpu.VMEM((48, width), jnp.bfloat16),
            pltpu.VMEM((32, 4 * LANES), jnp.bfloat16),
            pltpu.VMEM((BLOCK, width), jnp.bfloat16),
            pltpu.VMEM((BLOCK, width), jnp.bfloat16),
        ],
        input_output_aliases={3: 0},
        compiler_params=pltpu.CompilerParams(vmem_limit_bytes=VMEM_BYTES),
        name="finish",
    )(factors, targets, moved, tile)


def apply_kernel(moved_ref, tile_ref, product_ref):
    step = pl.program_id(0)
    chunks = range(tile_ref.shape[1] // LANES)
    part = jnp.concatenate([moved_ref[i] for i in range(moved_ref.shape[0])], axis=1)
    product = jnp.dot(part, tile_ref[...], preferred_element_type=jnp.float32)

    @pl.when(step == 0)
    def _():
        for chunk in chunks:
            product_ref[chunk] = product[:, chunk * LANES : (chunk + 1) * LANES]

    @pl.when(step > 0)
    def _():
        for chunk in chunks:
            product_ref[chunk] += product[:, chunk * LANES : (chunk + 1) * LANES]


def apply(moved, tile, depth=1024):
    count, width = tile.shape
    onsets = moved.shape[1]
    return pl.pallas_call(
        apply_kernel,
        grid=(count // depth,),
        in_specs=[
            pl.BlockSpec((depth // LANES, onsets, LANES), lambda i: (i, 0, 0)),
            pl.BlockSpec((depth, width), lambda i: (i, 0)),
        ],
        out_specs=pl.BlockSpec((width // LANES, onsets, LANES), lambda i: (0, 0, 0)),
        out_shape=jax.ShapeDtypeStruct((width // LANES, onsets, LANES), jnp.float32),
        compiler_params=pltpu.CompilerParams(vmem_limit_bytes=VMEM_BYTES),
        name="apply",
    )(moved, tile)


def per_device(centers, normals, areas, onset, start):
    row_count = lax.axis_size("row")
    col_count = lax.axis_size("col")
    row_index = lax.axis_index("row")
    col_index = lax.axis_index("col")
    own = start.shape[1]
    count = start.shape[0]
    own_first = col_index * own
    own_areas = lax.dynamic_slice_in_dim(areas, own_first, own, 0)
    own_normals = lax.dynamic_slice_in_dim(normals, own_first, own, 1)
    own_centers = lax.dynamic_slice_in_dim(centers, own_first, own, 1)

    mark = jnp.concatenate([jnp.ones((1, own)), jnp.zeros((4, own))], axis=0)
    note = jnp.concatenate([own_centers, mark.astype(jnp.float32)], axis=0)
    notes = spread(note, "row", row_count)
    shown = jnp.broadcast_to(start.astype(jnp.bfloat16)[None], (col_count, count, own))
    place = jnp.concatenate([centers, areas[None, :], jnp.zeros((4, areas.shape[0]))], axis=0)
    factors = source_factors(place, jnp.pad(normals, ((0, 5), (0, 0))))
    notes, shown, factors = lax.optimization_barrier((notes, shown, factors))
    targets = jnp.transpose(notes, (1, 0, 2)).reshape(8, row_count * own)
    moved = lax.all_to_all(shown, "col", 0, 0, tiled=True)

    tile = build(factors, targets)
    tile, partial = finish_build(factors, targets, moved, tile)

    product = jnp.sum(lax.all_to_all(partial, "row", 0, 0, tiled=True), axis=0)
    right = -jnp.sum(onset[:, :, None] * own_normals[:, None, :], axis=0)
    residual = right - 0.5 * start - product
    gathered = spread(residual.astype(jnp.bfloat16), "col", col_count)
    partial = apply(gathered, tile)
    change = jnp.sum(lax.all_to_all(partial, "row", 0, 0, tiled=True), axis=0)

    flat = row_index * col_count + col_index
    devices = row_count * col_count
    edges = jnp.concatenate([start, residual, change, own_centers], axis=0)
    forward = [(i, i + 1) for i in range(devices - 1)]
    backward = [(i + 1, i) for i in range(devices - 1)]
    before = lax.ppermute(edges[:, own - PB :], ("row", "col"), forward)
    after = lax.ppermute(edges[:, :PB], ("row", "col"), backward)

    weighted = own_areas[None, :] * residual
    part = jnp.concatenate(
        [
            jnp.sum(weighted * residual, axis=1),
            jnp.sum(weighted * change, axis=1),
            jnp.sum(own_areas[None, :] * change * change, axis=1),
            jnp.broadcast_to(jnp.sum(own_areas), (count,)),
        ]
    )
    part = jnp.broadcast_to(part[None, None], (col_count, 8, 4 * count))
    part = jnp.sum(lax.all_to_all(part, "col", 0, 0, tiled=True), axis=0)
    part = jnp.sum(spread(part, "row", row_count), axis=0)[0]
    both = part[:count]
    mixed = part[count : 2 * count]
    changed = part[2 * count : 3 * count]
    reach = CAP * jnp.sqrt(part[3 * count])

    def damp(sums):
        return OMEGA * jnp.minimum(1.0, reach * lax.rsqrt(sums + EPS))

    one = damp(both)
    keep = 1.0 - 0.5 * one
    sums = keep * keep * both - 2.0 * keep * one * mixed + one * one * changed
    two = damp(jnp.maximum(sums, 0.0))
    on_residual = (one + two * keep)[:, None]
    on_change = (two * one)[:, None]

    def finish(edge):
        strengths = edge[:count] + on_residual * edge[count : 2 * count]
        strengths = strengths - on_change * edge[2 * count : 3 * count]
        return jnp.concatenate([strengths, edge[3 * count :]], axis=0)

    fields = finish(edges)
    state = fields[:count]
    before = jnp.where(flat == 0, fields[:, :PB], finish(before))
    after = jnp.where(flat == devices - 1, fields[:, own - PB :], finish(after))
    padded = jnp.concatenate([before, fields, after], axis=1)
    diff_a = padded[:, 2 * PB :] - padded[:, :own]
    lane = lax.broadcasted_iota(jnp.int32, fields.shape, 1) % PB
    following = jnp.where(lane == PB - 1, jnp.roll(fields, PB - 1, 1), jnp.roll(fields, -1, 1))
    preceding = jnp.where(lane == 0, jnp.roll(fields, 1 - PB, 1), jnp.roll(fields, 1, 1))
    diff_b = following - preceding
    speeds = []
    for diff in (diff_a, diff_b):
        step = diff[count:]
        span = jnp.sqrt(jnp.sum(step * step, axis=0))
        along = jnp.sum(onset[:, :, None] * step[:, None, :], axis=0)
        speeds.append(along / span - diff[:count] / span)
    pressure = 1.0 - speeds[0] * speeds[0] - speeds[1] * speeds[1]
    return (state, pressure)


def solution(mesh):
    return jax.shard_map(
        per_device,
        mesh=mesh,
        in_specs=(P(None, "row"), P(None, "row"), P("row"), P(), P(None, ("row", "col"))),
        out_specs=(P(None, ("row", "col")), P(None, ("row", "col"))),
        check_vma=False,
    )
```

```python
import math

import jax
import jax.numpy as jnp
from jax import lax
from jax.experimental import pallas as pl
from jax.experimental.pallas import tpu as pltpu
from jax.sharding import PartitionSpec as P

PB = 32
SWEEPS = 2


INV_FOUR_PI = 1.0 / (4.0 * math.pi)
CAP = 0.4
OMEGA = 1.5
EPS = 1e-06
LANES = 128
STEP = 256
BLOCK = 512
VMEM_BYTES = 58 << 20
FINISH_BYTES = 50 << 20
SMALL_BYTES = 4 << 20


def spread(block, axis, count):
    copies = jnp.broadcast_to(block[None], (count,) + block.shape)
    return lax.all_to_all(copies, axis, 0, 0, tiled=True)


def three(value):
    high = value.astype(jnp.bfloat16).astype(jnp.float32)
    rest = value - high
    middle = rest.astype(jnp.bfloat16).astype(jnp.float32)
    return high, middle, rest - middle


def factor_kernel(center_ref, normal_ref, area_ref, factor_ref):
    width = center_ref.shape[1]
    blank = jnp.zeros((4, width), jnp.float32)
    area = area_ref[...]
    place = jnp.concatenate([center_ref[...], area, blank], axis=0)
    scaled = normal_ref[...] * (area * INV_FOUR_PI)
    level = -jnp.sum(scaled * center_ref[...], axis=0, keepdims=True)
    high, middle, low = three(jnp.concatenate([scaled, level, blank], axis=0))
    at_level = lax.broadcasted_iota(jnp.int32, high.shape, 0) == 3
    bare = jnp.where(at_level, 0.0, high)
    bare_middle = jnp.where(at_level, 0.0, middle)
    none = jnp.zeros_like(high)
    rows = [high, bare, middle, bare, bare_middle, low, none, none]
    rows += list(three(place)) + [none] * 5
    factor_ref[...] = jnp.concatenate(rows, axis=0).T.astype(jnp.bfloat16)


def source_factors(centers, normals, areas, block=1024):
    count = centers.shape[1]
    return pl.pallas_call(
        factor_kernel,
        grid=(count // block,),
        in_specs=[
            pl.BlockSpec((3, block), lambda i: (0, i)),
            pl.BlockSpec((3, block), lambda i: (0, i)),
            pl.BlockSpec((1, block), lambda i: (0, i)),
        ],
        out_specs=pl.BlockSpec((block, LANES), lambda i: (i, 0)),
        out_shape=jax.ShapeDtypeStruct((count, LANES), jnp.bfloat16),
        cost_estimate=pl.CostEstimate(
            flops=count * 400, bytes_accessed=count * 320, transcendentals=0
        ),
        name="factors",
    )(centers, normals, areas[None, :])


def target_factors(targets):
    high = targets.astype(jnp.bfloat16).astype(jnp.float32)
    rest = targets - high
    middle = rest.astype(jnp.bfloat16).astype(jnp.float32)
    low = rest - middle
    rows = [high, middle, high, low, middle, high]
    return jnp.concatenate(rows, axis=0).astype(jnp.bfloat16)


def fill(factor_ref, target_ref, wide_ref, pair_ref, column, stores):
    facing = jnp.dot(
        factor_ref[:, :48],
        pair_ref[:, column : column + STEP],
        preferred_element_type=jnp.float32,
    )
    for lane in range(0, STEP, LANES):
        here = slice(column + lane, column + lane + LANES)
        x, y, z = (target_ref[d : d + 1, here] for d in range(3))
        for row in range(0, BLOCK, 16):
            at = slice(row, row + 16)
            delta_x = x - wide_ref[0, at, :]
            delta_y = y - wide_ref[1, at, :]
            delta_z = z - wide_ref[2, at, :]
            dist_sq = delta_x * delta_x + delta_y * delta_y + delta_z * delta_z + wide_ref[3, at, :]
            inverse = lax.rsqrt(dist_sq)
            value = facing[row : row + 16, lane : lane + LANES] * (inverse * inverse * inverse)
            value = value.astype(jnp.bfloat16)
            for store in stores:
                store[at, here] = value


def prepare(target_ref, pair_ref, spread_ref):
    pair_ref[...] = target_factors(target_ref[...])
    which = lax.broadcasted_iota(jnp.int32, spread_ref.shape, 0)
    lane = lax.broadcasted_iota(jnp.int32, spread_ref.shape, 1)
    chosen = which % 8 == lane // LANES
    spread_ref[...] = jnp.where(chosen, 1.0, 0.0).astype(jnp.bfloat16)


def spread_params(factor_ref, spread_ref, wide_ref):
    wide = jnp.dot(factor_ref[:, 64:96], spread_ref[...], preferred_element_type=jnp.float32)
    for row in range(4):
        wide_ref[row] = wide[:, row * LANES : (row + 1) * LANES]


def build_kernel(factor_ref, target_ref, tile_ref, wide_ref, pair_ref, spread_ref):
    @pl.when(pl.program_id(0) == 0)
    def _():
        prepare(target_ref, pair_ref, spread_ref)

    spread_params(factor_ref, spread_ref, wide_ref)
    for column in range(0, tile_ref.shape[1], STEP):
        fill(factor_ref, target_ref, wide_ref, pair_ref, column, [tile_ref])


def finish_kernel(
    factor_ref,
    target_ref,
    moved_ref,
    old_ref,
    tile_ref,
    product_ref,
    wide_ref,
    pair_ref,
    spread_ref,
    even_ref,
    odd_ref,
):
    step = pl.program_id(0)
    blocks = pl.num_programs(0) - 1
    width = tile_ref.shape[1]
    deep = BLOCK // LANES

    @pl.when(step == 0)
    def _():
        prepare(target_ref, pair_ref, spread_ref)
        product_ref[...] = jnp.zeros_like(product_ref)

    def dot(block, ref, column):
        part = jnp.concatenate([moved_ref[deep * block + i] for i in range(deep)], axis=1)
        return jnp.dot(
            part, ref[:, column : column + STEP], preferred_element_type=jnp.float32
        )

    def add_to(column, value):
        for lane in range(0, STEP, LANES):
            product_ref[(column + lane) // LANES] += value[:, lane : lane + LANES]

    def whole(now_ref, before_ref):
        spread_params(factor_ref, spread_ref, wide_ref)
        for column in range(0, width, STEP):
            value = dot(step, old_ref, column)
            if before_ref is not None:
                value += dot(blocks + step - 1, before_ref, column)
            fill(
                factor_ref, target_ref, wide_ref, pair_ref, column, [tile_ref, now_ref]
            )
            add_to(column, value)

    @pl.when(step == 0)
    def _():
        whole(even_ref, None)

    @pl.when((step > 0) & (step < blocks) & (step % 2 == 0))
    def _():
        whole(even_ref, odd_ref)

    @pl.when((step < blocks) & (step % 2 == 1))
    def _():
        whole(odd_ref, even_ref)

    @pl.when((step == blocks) & (step % 2 == 0))
    def _():
        for column in range(0, width, STEP):
            add_to(column, dot(blocks + step - 1, odd_ref, column))

    @pl.when((step == blocks) & (step % 2 == 1))
    def _():
        for column in range(0, width, STEP):
            add_to(column, dot(blocks + step - 1, even_ref, column))


def build(factors, targets):
    count = factors.shape[0]
    width = targets.shape[1]
    return pl.pallas_call(
        build_kernel,
        grid=(count // BLOCK // 2,),
        in_specs=[
            pl.BlockSpec((BLOCK, LANES), lambda i: (i, 0)),
            pl.BlockSpec((8, width), lambda i: (0, 0)),
        ],
        out_specs=pl.BlockSpec((BLOCK, width), lambda i: (i, 0)),
        out_shape=pltpu.HBM((count, width), jnp.bfloat16),
        scratch_shapes=[
            pltpu.VMEM((4, BLOCK, LANES), jnp.float32),
            pltpu.VMEM((48, width), jnp.bfloat16),
            pltpu.VMEM((32, 4 * LANES), jnp.bfloat16),
        ],
        compiler_params=pltpu.CompilerParams(vmem_limit_bytes=VMEM_BYTES),
        cost_estimate=pl.CostEstimate(
            flops=count * width * 50, bytes_accessed=count * width, transcendentals=count * width // 2
        ),
        name="build",
    )(factors, targets)


def finish_build(factors, targets, moved, tile):
    count, width = tile.shape
    blocks = count // BLOCK // 2
    onsets = moved.shape[1]
    return pl.pallas_call(
        finish_kernel,
        grid=(blocks + 1,),
        in_specs=[
            pl.BlockSpec((BLOCK, LANES), lambda i: (blocks + jnp.minimum(i, blocks - 1), 0)),
            pl.BlockSpec((8, width), lambda i: (0, 0)),
            pl.BlockSpec(moved.shape, lambda i: (0, 0, 0)),
            pl.BlockSpec((BLOCK, width), lambda i: (jnp.minimum(i, blocks - 1), 0)),
        ],
        out_specs=[
            pl.BlockSpec((BLOCK, width), lambda i: (blocks + jnp.minimum(i, blocks - 1), 0)),
            pl.BlockSpec((width // LANES, onsets, LANES), lambda i: (0, 0, 0)),
        ],
        out_shape=[
            pltpu.HBM((count, width), jnp.bfloat16),
            jax.ShapeDtypeStruct((width // LANES, onsets, LANES), jnp.float32),
        ],
        scratch_shapes=[
            pltpu.VMEM((4, BLOCK, LANES), jnp.float32),
            pltpu.VMEM((48, width), jnp.bfloat16),
            pltpu.VMEM((32, 4 * LANES), jnp.bfloat16),
            pltpu.VMEM((BLOCK, width), jnp.bfloat16),
            pltpu.VMEM((BLOCK, width), jnp.bfloat16),
        ],
        input_output_aliases={3: 0},
        compiler_params=pltpu.CompilerParams(vmem_limit_bytes=FINISH_BYTES),
        name="finish",
    )(factors, targets, moved, tile)


def apply_kernel(moved_ref, tile_ref, product_ref):
    step = pl.program_id(0)
    chunks = range(tile_ref.shape[1] // LANES)
    part = jnp.concatenate([moved_ref[i] for i in range(moved_ref.shape[0])], axis=1)
    product = jnp.dot(part, tile_ref[...], preferred_element_type=jnp.float32)

    @pl.when(step == 0)
    def _():
        for chunk in chunks:
            product_ref[chunk] = product[:, chunk * LANES : (chunk + 1) * LANES]

    @pl.when(step > 0)
    def _():
        for chunk in chunks:
            product_ref[chunk] += product[:, chunk * LANES : (chunk + 1) * LANES]


def apply(moved, tile, depth=1024):
    count, width = tile.shape
    onsets = moved.shape[1]
    return pl.pallas_call(
        apply_kernel,
        grid=(count // depth,),
        in_specs=[
            pl.BlockSpec((depth // LANES, onsets, LANES), lambda i: (i, 0, 0)),
            pl.BlockSpec((depth, width), lambda i: (i, 0)),
        ],
        out_specs=pl.BlockSpec((width // LANES, onsets, LANES), lambda i: (0, 0, 0)),
        out_shape=jax.ShapeDtypeStruct((width // LANES, onsets, LANES), jnp.float32),
        compiler_params=pltpu.CompilerParams(vmem_limit_bytes=VMEM_BYTES),
        name="apply",
    )(moved, tile)


def residual_kernel(part_ref, base_ref, residual_ref, sent_ref):
    residual = base_ref[...] - jnp.sum(part_ref[...], axis=0)
    residual_ref[...] = residual
    sent = residual.astype(jnp.bfloat16)
    for device in range(sent_ref.shape[0]):
        sent_ref[device] = sent


def residual_of(parts, base, devices):
    return pl.pallas_call(
        residual_kernel,
        in_specs=[WHOLE] * 2,
        out_specs=[WHOLE] * 2,
        out_shape=[
            jax.ShapeDtypeStruct(base.shape, jnp.float32),
            jax.ShapeDtypeStruct((devices,) + base.shape, jnp.bfloat16),
        ],
        compiler_params=pltpu.CompilerParams(vmem_limit_bytes=SMALL_BYTES),
        name="residual",
    )(parts, base)


def sums_kernel(part_ref, start_ref, residual_ref, center_ref, area_ref, field_ref, sent_ref):
    change = jnp.sum(part_ref[...], axis=0)
    residual = residual_ref[...]
    count = residual.shape[0]
    field_ref[:count] = start_ref[...]
    field_ref[count : 2 * count] = residual
    field_ref[2 * count : 3 * count] = change
    field_ref[3 * count :] = center_ref[...]
    area = jnp.broadcast_to(area_ref[...], residual.shape)
    weighted = area * residual
    terms = [weighted * residual, weighted * change, area * change * change, area]
    total = jnp.sum(jnp.concatenate(terms, axis=0).T, axis=0, keepdims=True)
    sent = jnp.broadcast_to(total, sent_ref.shape[1:])
    for device in range(sent_ref.shape[0]):
        sent_ref[device] = sent


def sums_of(parts, start, residual, centers, areas, devices):
    count, own = start.shape
    return pl.pallas_call(
        sums_kernel,
        in_specs=[WHOLE] * 5,
        out_specs=[WHOLE] * 2,
        out_shape=[
            jax.ShapeDtypeStruct((3 * count + 8, own), jnp.float32),
            jax.ShapeDtypeStruct((devices, 8, 4 * count), jnp.float32),
        ],
        compiler_params=pltpu.CompilerParams(vmem_limit_bytes=SMALL_BYTES),
        name="sums",
    )(parts, start, residual, centers, areas)


def regroup_kernel(part_ref, sent_ref):
    sent = jnp.sum(part_ref[...], axis=0)
    for device in range(sent_ref.shape[0]):
        sent_ref[device] = sent


def regroup(parts, devices):
    return pl.pallas_call(
        regroup_kernel,
        in_specs=[WHOLE],
        out_specs=WHOLE,
        out_shape=jax.ShapeDtypeStruct((devices,) + parts.shape[1:], jnp.float32),
        compiler_params=pltpu.CompilerParams(vmem_limit_bytes=SMALL_BYTES),
        name="regroup",
    )(parts)


def last_kernel(
    part_ref, field_ref, before_ref, after_ref, onset_ref, end_ref, state_ref, pressure_ref
):
    count, own = state_ref.shape
    total = jnp.sum(part_ref[...], axis=0)[0:1, :]
    total = jnp.broadcast_to(total, (4 * count, own)).T
    both, mixed, changed, area = (total[i * count : (i + 1) * count] for i in range(4))
    reach = CAP * jnp.sqrt(area)

    def damp(sums):
        return OMEGA * jnp.minimum(1.0, reach * lax.rsqrt(sums + EPS))

    one = damp(both)
    keep = 1.0 - 0.5 * one
    sums = keep * keep * both - 2.0 * keep * one * mixed + one * one * changed
    two = damp(jnp.maximum(sums, 0.0))
    on_residual = one + two * keep
    on_change = two * one

    def strengths(ref):
        value = ref[:count] + on_residual * ref[count : 2 * count]
        return value - on_change * ref[2 * count : 3 * count]

    state = strengths(field_ref)
    state_ref[...] = state

    def differences(middle, low, high):
        lane = lax.broadcasted_iota(jnp.int32, middle.shape, 1)
        is_first = jnp.broadcast_to(end_ref[0], middle.shape) == 1
        is_last = jnp.broadcast_to(end_ref[1], middle.shape) == 1
        low = jnp.where(is_first, middle, pltpu.roll(low, PB, 1))
        high = jnp.where(is_last, middle, pltpu.roll(high, own - PB, 1))
        lower = jnp.where(lane < PB, low, pltpu.roll(middle, PB, 1))
        upper = jnp.where(lane >= own - PB, high, pltpu.roll(middle, own - PB, 1))
        around = lane % PB
        following = jnp.where(
            around == PB - 1, pltpu.roll(middle, PB - 1, 1), pltpu.roll(middle, own - 1, 1)
        )
        preceding = jnp.where(
            around == 0, pltpu.roll(middle, own - PB + 1, 1), pltpu.roll(middle, 1, 1)
        )
        return upper - lower, following - preceding

    steps = differences(field_ref[3 * count :], before_ref[3 * count :], after_ref[3 * count :])
    changes = differences(state, strengths(before_ref), strengths(after_ref))
    pressure = jnp.ones_like(state)
    for step, change in zip(steps, changes):
        span = jnp.sqrt(jnp.sum(step * step, axis=0, keepdims=True))
        along = onset_ref[:, 0:1] * step[0:1]
        along += onset_ref[:, 1:2] * step[1:2]
        along += onset_ref[:, 2:3] * step[2:3]
        speed = along / span - change / span
        pressure -= speed * speed
    pressure_ref[...] = pressure


def last(parts, fields, before, after, onset, ends, count):
    own = fields.shape[1]
    return pl.pallas_call(
        last_kernel,
        in_specs=[WHOLE] * 5 + [pl.BlockSpec(memory_space=pltpu.SMEM)],
        out_specs=[WHOLE] * 2,
        out_shape=[jax.ShapeDtypeStruct((count, own), jnp.float32)] * 2,
        compiler_params=pltpu.CompilerParams(vmem_limit_bytes=SMALL_BYTES),
        name="last",
    )(parts, fields, before, after, onset, ends)


WHOLE = pl.BlockSpec(memory_space=pltpu.VMEM)


def per_device(centers, normals, areas, onset, start):
    row_count = lax.axis_size("row")
    col_count = lax.axis_size("col")
    row_index = lax.axis_index("row")
    col_index = lax.axis_index("col")
    own = start.shape[1]
    count = start.shape[0]
    own_first = col_index * own
    own_areas = lax.dynamic_slice_in_dim(areas, own_first, own, 0)
    own_normals = lax.dynamic_slice_in_dim(normals, own_first, own, 1)
    own_centers = lax.dynamic_slice_in_dim(centers, own_first, own, 1)

    mark = jnp.concatenate([jnp.ones((1, own)), jnp.zeros((4, own))], axis=0)
    note = jnp.concatenate([own_centers, mark.astype(jnp.float32)], axis=0)
    notes = spread(note, "row", row_count)
    shown = jnp.broadcast_to(start.astype(jnp.bfloat16)[None], (col_count, count, own))
    factors = source_factors(centers, normals, areas)
    notes, shown, factors = lax.optimization_barrier((notes, shown, factors))
    targets = jnp.transpose(notes, (1, 0, 2)).reshape(8, row_count * own)
    moved = lax.all_to_all(shown, "col", 0, 0, tiled=True)

    tile = build(factors, targets)
    tile, partial = finish_build(factors, targets, moved, tile)

    right = -jnp.sum(onset[:, :, None] * own_normals[:, None, :], axis=0)
    base = right - 0.5 * start
    parts = lax.all_to_all(partial, "row", 0, 0, tiled=True)
    residual, sent = residual_of(parts, base, col_count)
    gathered = lax.all_to_all(sent, "col", 0, 0, tiled=True)
    partial = apply(gathered, tile)
    parts = lax.all_to_all(partial, "row", 0, 0, tiled=True)
    here = jnp.pad(own_centers, ((0, 5), (0, 0)))
    fields, sent = sums_of(parts, start, residual, here, own_areas[None, :], col_count)

    flat = row_index * col_count + col_index
    devices = row_count * col_count
    forward = [(i, i + 1) for i in range(devices - 1)]
    backward = [(i + 1, i) for i in range(devices - 1)]
    parts = lax.all_to_all(sent, "col", 0, 0, tiled=True)
    before = lax.ppermute(fields, ("row", "col"), forward)
    after = lax.ppermute(fields, ("row", "col"), backward)
    parts, before, after = lax.optimization_barrier((parts, before, after))
    parts = lax.all_to_all(regroup(parts, row_count), "row", 0, 0, tiled=True)
    ends = jnp.stack([flat == 0, flat == devices - 1]).astype(jnp.int32)
    return last(parts, fields, before, after, onset.T, ends, count)


def solution(mesh):
    return jax.shard_map(
        per_device,
        mesh=mesh,
        in_specs=(P(None, "row"), P(None, "row"), P("row"), P(), P(None, ("row", "col"))),
        out_specs=(P(None, ("row", "col")), P(None, ("row", "col"))),
        check_vma=False,
    )
```

```python
import math

import jax
import jax.numpy as jnp
from jax import lax
from jax.experimental import pallas as pl
from jax.experimental.pallas import tpu as pltpu
from jax.sharding import PartitionSpec as P

PB = 32
SWEEPS = 2


INV_FOUR_PI = 1.0 / (4.0 * math.pi)
CAP = 0.4
OMEGA = 1.5
EPS = 1e-06
LANES = 128
STEP = 256
SIDES = 2
CORES = 2
BLOCK = 512
VMEM_BYTES = 58 << 20
FINISH_BYTES = 50 << 20
SMALL_BYTES = 4 << 20


def three(value):
    high = value.astype(jnp.bfloat16).astype(jnp.float32)
    rest = value - high
    middle = rest.astype(jnp.bfloat16).astype(jnp.float32)
    return high, middle, rest - middle


def note_kernel(at_ref, *refs):
    note_ref = refs[-1]
    halves = []
    for center_ref, normal_ref, area_ref in zip(refs[0:2], refs[2:4], refs[4:6]):
        center, area = center_ref[...], area_ref[...]
        scaled = normal_ref[...] * (area * INV_FOUR_PI)
        level = -jnp.sum(scaled * center, axis=0, keepdims=True)
        halves.append(jnp.concatenate([center, area, scaled, level], axis=0))
    note = jnp.concatenate(halves, axis=1)
    for device in range(note_ref.shape[0]):
        note_ref[device] = note


def notes_of(starts, centers, normals, areas, devices):
    def specs(rows):
        return [
            pl.BlockSpec((rows, LANES), lambda i, at, which=which: (0, at[which]))
            for which in (0, 1)
        ]

    return pl.pallas_call(
        note_kernel,
        grid_spec=pltpu.PrefetchScalarGridSpec(
            num_scalar_prefetch=1,
            grid=(1,),
            in_specs=specs(3) + specs(3) + specs(1),
            out_specs=pl.BlockSpec((devices, 8, 2 * LANES), lambda i, at: (0, 0, 0)),
        ),
        out_shape=jax.ShapeDtypeStruct((devices, 8, 2 * LANES), jnp.float32),
        compiler_params=pltpu.CompilerParams(vmem_limit_bytes=VMEM_BYTES),
        name="notes",
    )(starts, centers, centers, normals, normals, areas, areas)


def source_factors(note_ref):
    notes = jnp.concatenate([note_ref[i] for i in range(note_ref.shape[0])], axis=1)
    row = lax.broadcasted_iota(jnp.int32, notes.shape, 0)
    place = jnp.where(row < 4, notes, 0.0)
    high, middle, low = three(jnp.where(row < 4, pltpu.roll(notes, 4, 0), 0.0))
    bare = jnp.where(row == 3, 0.0, high)
    bare_middle = jnp.where(row == 3, 0.0, middle)
    none = jnp.zeros_like(high)
    rows = [high, bare, middle, bare, bare_middle, low, none, none]
    rows += list(three(place)) + [none] * 5
    return jnp.concatenate(rows, axis=0).T.astype(jnp.bfloat16)


def target_factors(targets):
    high = targets.astype(jnp.bfloat16).astype(jnp.float32)
    rest = targets - high
    middle = rest.astype(jnp.bfloat16).astype(jnp.float32)
    low = rest - middle
    rows = [high, middle, high, low, middle, high]
    return jnp.concatenate(rows, axis=0).astype(jnp.bfloat16)


def fill(factor_ref, target_ref, wide_ref, pair_ref, column, stores):
    facing = jnp.dot(
        factor_ref[:, :48],
        pair_ref[:, column : column + STEP],
        preferred_element_type=jnp.float32,
    )
    for lane in range(0, STEP, LANES):
        here = slice(column + lane, column + lane + LANES)
        x, y, z = (target_ref[d : d + 1, here] for d in range(3))
        for row in range(0, BLOCK, 16):
            at = slice(row, row + 16)
            delta_x = x - wide_ref[0, at, :]
            delta_y = y - wide_ref[1, at, :]
            delta_z = z - wide_ref[2, at, :]
            dist_sq = delta_x * delta_x + delta_y * delta_y + delta_z * delta_z + wide_ref[3, at, :]
            inverse = lax.rsqrt(dist_sq)
            value = facing[row : row + 16, lane : lane + LANES] * (inverse * inverse * inverse)
            value = value.astype(jnp.bfloat16)
            for store in stores:
                store[at, here] = value


def prepare(target_ref, pair_ref, spread_ref):
    pair_ref[...] = target_factors(target_ref[...])
    which = lax.broadcasted_iota(jnp.int32, spread_ref.shape, 0)
    lane = lax.broadcasted_iota(jnp.int32, spread_ref.shape, 1)
    chosen = which % 8 == lane // LANES
    spread_ref[...] = jnp.where(chosen, 1.0, 0.0).astype(jnp.bfloat16)


def spread_params(factor_ref, spread_ref, wide_ref):
    wide = jnp.dot(factor_ref[:, 64:96], spread_ref[...], preferred_element_type=jnp.float32)
    for row in range(4):
        wide_ref[row] = wide[:, row * LANES : (row + 1) * LANES]


def build_kernel(note_ref, target_ref, tile_ref, wide_ref, pair_ref, spread_ref, factor_ref):
    @pl.when(pl.program_id(0) == 0)
    def _():
        prepare(target_ref, pair_ref, spread_ref)

    factor_ref[...] = source_factors(note_ref)
    spread_params(factor_ref, spread_ref, wide_ref)
    for column in range(0, tile_ref.shape[1], STEP):
        fill(factor_ref, target_ref, wide_ref, pair_ref, column, [tile_ref])


def finish_kernel(
    note_ref,
    target_ref,
    moved_ref,
    old_ref,
    tile_ref,
    product_ref,
    wide_ref,
    pair_ref,
    spread_ref,
    factor_ref,
    even_ref,
    odd_ref,
):
    step = pl.program_id(0)
    blocks = pl.num_programs(0) - 1
    width = tile_ref.shape[1]
    deep = BLOCK // LANES

    @pl.when(step == 0)
    def _():
        prepare(target_ref, pair_ref, spread_ref)
        product_ref[...] = jnp.zeros_like(product_ref)

    def dot(block, ref, column):
        part = jnp.concatenate([moved_ref[deep * block + i] for i in range(deep)], axis=1)
        return jnp.dot(
            part, ref[:, column : column + STEP], preferred_element_type=jnp.float32
        )

    def add_to(column, value):
        for lane in range(0, STEP, LANES):
            product_ref[(column + lane) // LANES] += value[:, lane : lane + LANES]

    def whole(now_ref, before_ref):
        factor_ref[...] = source_factors(note_ref)
        spread_params(factor_ref, spread_ref, wide_ref)
        for column in range(0, width, STEP):
            value = dot(step, old_ref, column)
            if before_ref is not None:
                value += dot(blocks + step - 1, before_ref, column)
            fill(
                factor_ref, target_ref, wide_ref, pair_ref, column, [tile_ref, now_ref]
            )
            add_to(column, value)

    @pl.when(step == 0)
    def _():
        whole(even_ref, None)

    @pl.when((step > 0) & (step < blocks) & (step % 2 == 0))
    def _():
        whole(even_ref, odd_ref)

    @pl.when((step < blocks) & (step % 2 == 1))
    def _():
        whole(odd_ref, even_ref)

    @pl.when((step == blocks) & (step % 2 == 0))
    def _():
        for column in range(0, width, STEP):
            add_to(column, dot(blocks + step - 1, odd_ref, column))

    @pl.when((step == blocks) & (step % 2 == 1))
    def _():
        for column in range(0, width, STEP):
            add_to(column, dot(blocks + step - 1, even_ref, column))


def build(notes, targets):
    count = notes.shape[0] * notes.shape[2]
    width = targets.shape[1]
    return pl.pallas_call(
        build_kernel,
        grid=(count // BLOCK // 2,),
        in_specs=[
            pl.BlockSpec((BLOCK // 256, 8, 256), lambda i: (i, 0, 0)),
            pl.BlockSpec((8, width), lambda i: (0, 0)),
        ],
        out_specs=pl.BlockSpec((BLOCK, width), lambda i: (i, 0)),
        out_shape=pltpu.HBM((count, width), jnp.bfloat16),
        scratch_shapes=[
            pltpu.VMEM((4, BLOCK, LANES), jnp.float32),
            pltpu.VMEM((48, width), jnp.bfloat16),
            pltpu.VMEM((32, 4 * LANES), jnp.bfloat16),
            pltpu.VMEM((BLOCK, LANES), jnp.bfloat16),
        ],
        compiler_params=pltpu.CompilerParams(vmem_limit_bytes=VMEM_BYTES),
        cost_estimate=pl.CostEstimate(
            flops=count * width * 50, bytes_accessed=count * width, transcendentals=count * width // 2
        ),
        name="build",
    )(notes, targets)


def finish_build(notes, targets, moved, tile):
    count, width = tile.shape
    blocks = count // BLOCK // 2
    onsets = moved.shape[1]
    return pl.pallas_call(
        finish_kernel,
        grid=(blocks + 1,),
        in_specs=[
            pl.BlockSpec(
                (BLOCK // 256, 8, 256), lambda i: (blocks + jnp.minimum(i, blocks - 1), 0, 0)
            ),
            pl.BlockSpec((8, width), lambda i: (0, 0)),
            pl.BlockSpec(moved.shape, lambda i: (0, 0, 0)),
            pl.BlockSpec((BLOCK, width), lambda i: (jnp.minimum(i, blocks - 1), 0)),
        ],
        out_specs=[
            pl.BlockSpec((BLOCK, width), lambda i: (blocks + jnp.minimum(i, blocks - 1), 0)),
            pl.BlockSpec((width // LANES, onsets, LANES), lambda i: (0, 0, 0)),
        ],
        out_shape=[
            pltpu.HBM((count, width), jnp.bfloat16),
            jax.ShapeDtypeStruct((width // LANES, onsets, LANES), jnp.float32),
        ],
        scratch_shapes=[
            pltpu.VMEM((4, BLOCK, LANES), jnp.float32),
            pltpu.VMEM((48, width), jnp.bfloat16),
            pltpu.VMEM((32, 4 * LANES), jnp.bfloat16),
            pltpu.VMEM((BLOCK, LANES), jnp.bfloat16),
            pltpu.VMEM((BLOCK, width), jnp.bfloat16),
            pltpu.VMEM((BLOCK, width), jnp.bfloat16),
        ],
        input_output_aliases={3: 0},
        compiler_params=pltpu.CompilerParams(vmem_limit_bytes=FINISH_BYTES),
        name="finish",
    )(notes, targets, moved, tile)


def apply_kernel(moved_ref, tile_ref, product_ref):
    step = pl.program_id(0)
    chunks = range(tile_ref.shape[1] // LANES)
    part = jnp.concatenate([moved_ref[i] for i in range(moved_ref.shape[0])], axis=1)
    product = jnp.dot(part, tile_ref[...], preferred_element_type=jnp.float32)

    @pl.when(step == 0)
    def _():
        for chunk in chunks:
            product_ref[chunk] = product[:, chunk * LANES : (chunk + 1) * LANES]

    @pl.when(step > 0)
    def _():
        for chunk in chunks:
            product_ref[chunk] += product[:, chunk * LANES : (chunk + 1) * LANES]


def apply(moved, tile, depth=1024):
    count, width = tile.shape
    onsets = moved.shape[1]
    return pl.pallas_call(
        apply_kernel,
        grid=(count // depth,),
        in_specs=[
            pl.BlockSpec((depth // LANES, onsets, LANES), lambda i: (i, 0, 0)),
            pl.BlockSpec((depth, width), lambda i: (i, 0)),
        ],
        out_specs=pl.BlockSpec((width // LANES, onsets, LANES), lambda i: (0, 0, 0)),
        out_shape=jax.ShapeDtypeStruct((width // LANES, onsets, LANES), jnp.float32),
        compiler_params=pltpu.CompilerParams(vmem_limit_bytes=VMEM_BYTES),
        name="apply",
    )(moved, tile)


def residual_kernel(part_ref, base_ref, residual_ref, sent_ref):
    residual = base_ref[...] - jnp.sum(part_ref[...], axis=0)
    residual_ref[...] = residual
    sent = residual.astype(jnp.bfloat16)
    for device in range(sent_ref.shape[0]):
        sent_ref[device] = sent


def residual_of(parts, base, devices):
    return pl.pallas_call(
        residual_kernel,
        in_specs=[WHOLE] * 2,
        out_specs=[WHOLE] * 2,
        out_shape=[
            jax.ShapeDtypeStruct(base.shape, jnp.float32),
            jax.ShapeDtypeStruct((devices,) + base.shape, jnp.bfloat16),
        ],
        compiler_params=pltpu.CompilerParams(vmem_limit_bytes=SMALL_BYTES),
        name="residual",
    )(parts, base)


def sums_kernel(part_ref, start_ref, residual_ref, center_ref, area_ref, field_ref, sent_ref):
    change = jnp.sum(part_ref[...], axis=0)
    residual = residual_ref[...]
    count = residual.shape[0]
    field_ref[:count] = start_ref[...]
    field_ref[count : 2 * count] = residual
    field_ref[2 * count : 3 * count] = change
    field_ref[3 * count :] = center_ref[...]
    area = jnp.broadcast_to(area_ref[...], residual.shape)
    weighted = area * residual
    terms = [weighted * residual, weighted * change, area * change * change, area]
    total = jnp.sum(jnp.concatenate(terms, axis=0).T, axis=0, keepdims=True)
    sent = jnp.broadcast_to(total, sent_ref.shape[1:])
    for device in range(sent_ref.shape[0]):
        sent_ref[device] = sent


def sums_of(parts, start, residual, centers, areas, devices):
    count, own = start.shape
    return pl.pallas_call(
        sums_kernel,
        in_specs=[WHOLE] * 5,
        out_specs=[WHOLE] * 2,
        out_shape=[
            jax.ShapeDtypeStruct((3 * count + 8, own), jnp.float32),
            jax.ShapeDtypeStruct((devices, 8, 4 * count), jnp.float32),
        ],
        compiler_params=pltpu.CompilerParams(vmem_limit_bytes=SMALL_BYTES),
        name="sums",
    )(parts, start, residual, centers, areas)


def regroup_kernel(part_ref, sent_ref):
    sent = jnp.sum(part_ref[...], axis=0)
    for device in range(sent_ref.shape[0]):
        sent_ref[device] = sent


def regroup(parts, devices):
    return pl.pallas_call(
        regroup_kernel,
        in_specs=[WHOLE],
        out_specs=WHOLE,
        out_shape=jax.ShapeDtypeStruct((devices,) + parts.shape[1:], jnp.float32),
        compiler_params=pltpu.CompilerParams(vmem_limit_bytes=SMALL_BYTES),
        name="regroup",
    )(parts)


def last_kernel(
    part_ref, field_ref, before_ref, after_ref, onset_ref, end_ref, state_ref, pressure_ref
):
    count, own = state_ref.shape
    total = jnp.sum(part_ref[...], axis=0)[0:1, :]
    total = jnp.broadcast_to(total, (4 * count, own)).T
    both, mixed, changed, area = (total[i * count : (i + 1) * count] for i in range(4))
    reach = CAP * jnp.sqrt(area)

    def damp(sums):
        return OMEGA * jnp.minimum(1.0, reach * lax.rsqrt(sums + EPS))

    one = damp(both)
    keep = 1.0 - 0.5 * one
    sums = keep * keep * both - 2.0 * keep * one * mixed + one * one * changed
    two = damp(jnp.maximum(sums, 0.0))
    on_residual = one + two * keep
    on_change = two * one

    def strengths(ref):
        value = ref[:count] + on_residual * ref[count : 2 * count]
        return value - on_change * ref[2 * count : 3 * count]

    state = strengths(field_ref)
    state_ref[...] = state

    def differences(middle, low, high):
        lane = lax.broadcasted_iota(jnp.int32, middle.shape, 1)
        is_first = jnp.broadcast_to(end_ref[0], middle.shape) == 1
        is_last = jnp.broadcast_to(end_ref[1], middle.shape) == 1
        low = jnp.where(is_first, middle, pltpu.roll(low, PB, 1))
        high = jnp.where(is_last, middle, pltpu.roll(high, own - PB, 1))
        lower = jnp.where(lane < PB, low, pltpu.roll(middle, PB, 1))
        upper = jnp.where(lane >= own - PB, high, pltpu.roll(middle, own - PB, 1))
        around = lane % PB
        following = jnp.where(
            around == PB - 1, pltpu.roll(middle, PB - 1, 1), pltpu.roll(middle, own - 1, 1)
        )
        preceding = jnp.where(
            around == 0, pltpu.roll(middle, own - PB + 1, 1), pltpu.roll(middle, 1, 1)
        )
        return upper - lower, following - preceding

    steps = differences(field_ref[3 * count :], before_ref[3 * count :], after_ref[3 * count :])
    changes = differences(state, strengths(before_ref), strengths(after_ref))
    pressure = jnp.ones_like(state)
    for step, change in zip(steps, changes):
        span = jnp.sqrt(jnp.sum(step * step, axis=0, keepdims=True))
        along = onset_ref[:, 0:1] * step[0:1]
        along += onset_ref[:, 1:2] * step[1:2]
        along += onset_ref[:, 2:3] * step[2:3]
        speed = along / span - change / span
        pressure -= speed * speed
    pressure_ref[...] = pressure


def last(parts, fields, before, after, onset, ends, count):
    own = fields.shape[1]
    return pl.pallas_call(
        last_kernel,
        in_specs=[WHOLE] * 5 + [pl.BlockSpec(memory_space=pltpu.SMEM)],
        out_specs=[WHOLE] * 2,
        out_shape=[jax.ShapeDtypeStruct((count, own), jnp.float32)] * 2,
        compiler_params=pltpu.CompilerParams(vmem_limit_bytes=SMALL_BYTES),
        name="last",
    )(parts, fields, before, after, onset, ends)


WHOLE = pl.BlockSpec(memory_space=pltpu.VMEM)


def per_device(centers, normals, areas, onset, start):
    row_count = lax.axis_size("row")
    col_count = lax.axis_size("col")
    row_index = lax.axis_index("row")
    col_index = lax.axis_index("col")
    count, own = start.shape
    own_first = col_index * own
    own_areas = lax.dynamic_slice_in_dim(areas, own_first, own, 0)
    own_normals = lax.dynamic_slice_in_dim(normals, own_first, own, 1)
    own_centers = lax.dynamic_slice_in_dim(centers, own_first, own, 1)

    levels = col_count // (SIDES * CORES)
    z_index = col_index // (SIDES * CORES)
    y_index = col_index // CORES % SIDES
    core_index = col_index % CORES
    place = [
        [[(z * SIDES + y) * CORES + core for core in range(CORES)] for y in range(SIDES)]
        for z in range(levels)
    ]
    across = [
        [place[z][y][core] for z in range(levels) for core in range(CORES)] for y in range(SIDES)
    ]
    along = [
        [row * col_count + place[z][y][core] for row in range(row_count) for y in range(SIDES)]
        for z in range(levels)
        for core in range(CORES)
    ]

    def exchange_targets(value):
        return lax.all_to_all(value, "col", 0, 0, tiled=True, axis_index_groups=across)

    def exchange_sources(value):
        return lax.all_to_all(
            value, ("row", "col"), 0, 0, tiled=True, axis_index_groups=along
        )

    low = z_index * (SIDES * CORES) + core_index
    starts = jnp.stack([low, low + CORES]).astype(jnp.int32)
    notes = notes_of(starts, centers, normals, areas[None, :], row_count)
    notes = lax.all_to_all(notes, "row", 0, 0, tiled=True)
    shown = jnp.broadcast_to(
        start.astype(jnp.bfloat16)[None], (row_count * SIDES, count, own)
    )
    targets = lax.dynamic_index_in_dim(
        centers.reshape(3, levels, SIDES, CORES * own), y_index, 2, False
    ).reshape(3, levels * CORES * own)
    mark = jnp.ones((1, targets.shape[1]), jnp.float32)
    targets = jnp.concatenate([targets, mark, jnp.zeros((4, targets.shape[1]))], axis=0)
    right = -jnp.sum(onset[:, :, None] * own_normals[:, None, :], axis=0)
    base = right - 0.5 * start
    notes, shown, targets, base = lax.optimization_barrier((notes, shown, targets, base))
    moved = exchange_sources(shown)

    tile = build(notes, targets)
    tile, partial = finish_build(notes, targets, moved, tile)
    residual, sent = residual_of(exchange_targets(partial), base, row_count * SIDES)
    partial = apply(exchange_sources(sent), tile)
    parts = exchange_targets(partial)
    here = jnp.pad(own_centers, ((0, 5), (0, 0)))
    fields, sent = sums_of(parts, start, residual, here, own_areas[None, :], levels * CORES)

    flat = row_index * col_count + col_index
    devices = row_count * col_count
    forward = [(i, i + 1) for i in range(devices - 1)]
    backward = [(i + 1, i) for i in range(devices - 1)]
    parts = exchange_targets(sent)
    before = lax.ppermute(fields, ("row", "col"), forward)
    after = lax.ppermute(fields, ("row", "col"), backward)
    parts, before, after = lax.optimization_barrier((parts, before, after))
    parts = exchange_sources(regroup(parts, row_count * SIDES))
    ends = jnp.stack([flat == 0, flat == devices - 1]).astype(jnp.int32)
    return last(parts, fields, before, after, onset.T, ends, count)


def solution(mesh):
    return jax.shard_map(
        per_device,
        mesh=mesh,
        in_specs=(P(None, "row"), P(None, "row"), P("row"), P(), P(None, ("row", "col"))),
        out_specs=(P(None, ("row", "col")), P(None, ("row", "col"))),
        check_vma=False,
    )
```

```python
import math

import jax
import jax.numpy as jnp
from jax import lax
from jax.experimental import pallas as pl
from jax.experimental.pallas import tpu as pltpu
from jax.sharding import PartitionSpec as P

PB = 32
SWEEPS = 2


INV_FOUR_PI = 1.0 / (4.0 * math.pi)
CAP = 0.4
OMEGA = 1.5
EPS = 1e-06
LANES = 128
STEP = 256
BLOCK = 512
VMEM_BYTES = 58 << 20
FINISH_BYTES = 50 << 20
SMALL_BYTES = 4 << 20


def spread(block, axis, count):
    copies = jnp.broadcast_to(block[None], (count,) + block.shape)
    return lax.all_to_all(copies, axis, 0, 0, tiled=True)


def three(value):
    high = value.astype(jnp.bfloat16).astype(jnp.float32)
    rest = value - high
    middle = rest.astype(jnp.bfloat16).astype(jnp.float32)
    return high, middle, rest - middle


def factor_kernel(center_ref, normal_ref, area_ref, start_ref, factor_ref, shown_ref):
    @pl.when(pl.program_id(0) == 0)
    def _():
        shown = start_ref[...].astype(jnp.bfloat16)
        for device in range(shown_ref.shape[0]):
            shown_ref[device] = shown

    width = center_ref.shape[1]
    blank = jnp.zeros((4, width), jnp.float32)
    area = area_ref[...]
    place = jnp.concatenate([center_ref[...], area, blank], axis=0)
    scaled = normal_ref[...] * (area * INV_FOUR_PI)
    level = -jnp.sum(scaled * center_ref[...], axis=0, keepdims=True)
    high, middle, low = three(jnp.concatenate([scaled, level, blank], axis=0))
    at_level = lax.broadcasted_iota(jnp.int32, high.shape, 0) == 3
    bare = jnp.where(at_level, 0.0, high)
    bare_middle = jnp.where(at_level, 0.0, middle)
    none = jnp.zeros_like(high)
    rows = [high, bare, middle, bare, bare_middle, low, none, none]
    rows += list(three(place)) + [none] * 5
    factor_ref[...] = jnp.concatenate(rows, axis=0).T.astype(jnp.bfloat16)


def source_factors(centers, normals, areas, start, devices, block=1024):
    count = centers.shape[1]
    return pl.pallas_call(
        factor_kernel,
        grid=(count // block,),
        in_specs=[
            pl.BlockSpec((3, block), lambda i: (0, i)),
            pl.BlockSpec((3, block), lambda i: (0, i)),
            pl.BlockSpec((1, block), lambda i: (0, i)),
            pl.BlockSpec(start.shape, lambda i: (0, 0)),
        ],
        out_specs=[
            pl.BlockSpec((block, LANES), lambda i: (i, 0)),
            pl.BlockSpec((devices,) + start.shape, lambda i: (0, 0, 0)),
        ],
        out_shape=[
            jax.ShapeDtypeStruct((count, LANES), jnp.bfloat16),
            jax.ShapeDtypeStruct((devices,) + start.shape, jnp.bfloat16),
        ],
        cost_estimate=pl.CostEstimate(
            flops=count * 400, bytes_accessed=count * 400, transcendentals=0
        ),
        name="factors",
    )(centers, normals, areas[None, :], start)


def target_factors(targets):
    high = targets.astype(jnp.bfloat16).astype(jnp.float32)
    rest = targets - high
    middle = rest.astype(jnp.bfloat16).astype(jnp.float32)
    low = rest - middle
    rows = [high, middle, high, low, middle, high]
    return jnp.concatenate(rows, axis=0).astype(jnp.bfloat16)


def fill(factor_ref, target_ref, wide_ref, pair_ref, column, stores):
    facing = jnp.dot(
        factor_ref[:, :48],
        pair_ref[:, column : column + STEP],
        preferred_element_type=jnp.float32,
    )
    for lane in range(0, STEP, LANES):
        here = slice(column + lane, column + lane + LANES)
        x, y, z = (target_ref[d : d + 1, here] for d in range(3))
        for row in range(0, BLOCK, 16):
            at = slice(row, row + 16)
            delta_x = x - wide_ref[0, at, :]
            delta_y = y - wide_ref[1, at, :]
            delta_z = z - wide_ref[2, at, :]
            dist_sq = delta_x * delta_x + delta_y * delta_y + delta_z * delta_z + wide_ref[3, at, :]
            inverse = lax.rsqrt(dist_sq)
            value = facing[row : row + 16, lane : lane + LANES] * (inverse * inverse * inverse)
            value = value.astype(jnp.bfloat16)
            for store in stores:
                store[at, here] = value


def prepare(target_ref, pair_ref, spread_ref):
    pair_ref[...] = target_factors(target_ref[...])
    which = lax.broadcasted_iota(jnp.int32, spread_ref.shape, 0)
    lane = lax.broadcasted_iota(jnp.int32, spread_ref.shape, 1)
    chosen = which % 8 == lane // LANES
    spread_ref[...] = jnp.where(chosen, 1.0, 0.0).astype(jnp.bfloat16)


def spread_params(factor_ref, spread_ref, wide_ref):
    wide = jnp.dot(factor_ref[:, 64:96], spread_ref[...], preferred_element_type=jnp.float32)
    for row in range(4):
        wide_ref[row] = wide[:, row * LANES : (row + 1) * LANES]


def build_kernel(factor_ref, target_ref, tile_ref, wide_ref, pair_ref, spread_ref):
    @pl.when(pl.program_id(0) == 0)
    def _():
        prepare(target_ref, pair_ref, spread_ref)

    spread_params(factor_ref, spread_ref, wide_ref)
    for column in range(0, tile_ref.shape[1], STEP):
        fill(factor_ref, target_ref, wide_ref, pair_ref, column, [tile_ref])


def finish_kernel(
    factor_ref,
    target_ref,
    moved_ref,
    old_ref,
    tile_ref,
    product_ref,
    wide_ref,
    pair_ref,
    spread_ref,
    even_ref,
    odd_ref,
):
    step = pl.program_id(0)
    blocks = pl.num_programs(0) - 1
    width = tile_ref.shape[1]
    deep = BLOCK // LANES

    @pl.when(step == 0)
    def _():
        prepare(target_ref, pair_ref, spread_ref)
        product_ref[...] = jnp.zeros_like(product_ref)

    def dot(block, ref, column):
        part = jnp.concatenate([moved_ref[deep * block + i] for i in range(deep)], axis=1)
        return jnp.dot(
            part, ref[:, column : column + STEP], preferred_element_type=jnp.float32
        )

    def add_to(column, value):
        for lane in range(0, STEP, LANES):
            product_ref[(column + lane) // LANES] += value[:, lane : lane + LANES]

    def whole(now_ref, before_ref):
        spread_params(factor_ref, spread_ref, wide_ref)
        for column in range(0, width, STEP):
            value = dot(step, old_ref, column)
            if before_ref is not None:
                value += dot(blocks + step - 1, before_ref, column)
            fill(
                factor_ref, target_ref, wide_ref, pair_ref, column, [tile_ref, now_ref]
            )
            add_to(column, value)

    @pl.when(step == 0)
    def _():
        whole(even_ref, None)

    @pl.when((step > 0) & (step < blocks) & (step % 2 == 0))
    def _():
        whole(even_ref, odd_ref)

    @pl.when((step < blocks) & (step % 2 == 1))
    def _():
        whole(odd_ref, even_ref)

    @pl.when((step == blocks) & (step % 2 == 0))
    def _():
        for column in range(0, width, STEP):
            add_to(column, dot(blocks + step - 1, odd_ref, column))

    @pl.when((step == blocks) & (step % 2 == 1))
    def _():
        for column in range(0, width, STEP):
            add_to(column, dot(blocks + step - 1, even_ref, column))


def build(factors, targets):
    count = factors.shape[0]
    width = targets.shape[1]
    return pl.pallas_call(
        build_kernel,
        grid=(count // BLOCK // 2,),
        in_specs=[
            pl.BlockSpec((BLOCK, LANES), lambda i: (i, 0)),
            pl.BlockSpec((8, width), lambda i: (0, 0)),
        ],
        out_specs=pl.BlockSpec((BLOCK, width), lambda i: (i, 0)),
        out_shape=pltpu.HBM((count, width), jnp.bfloat16),
        scratch_shapes=[
            pltpu.VMEM((4, BLOCK, LANES), jnp.float32),
            pltpu.VMEM((48, width), jnp.bfloat16),
            pltpu.VMEM((32, 4 * LANES), jnp.bfloat16),
        ],
        compiler_params=pltpu.CompilerParams(vmem_limit_bytes=VMEM_BYTES),
        cost_estimate=pl.CostEstimate(
            flops=count * width * 50, bytes_accessed=count * width, transcendentals=count * width // 2
        ),
        name="build",
    )(factors, targets)


def finish_build(factors, targets, moved, tile):
    count, width = tile.shape
    blocks = count // BLOCK // 2
    onsets = moved.shape[1]
    return pl.pallas_call(
        finish_kernel,
        grid=(blocks + 1,),
        in_specs=[
            pl.BlockSpec((BLOCK, LANES), lambda i: (blocks + jnp.minimum(i, blocks - 1), 0)),
            pl.BlockSpec((8, width), lambda i: (0, 0)),
            pl.BlockSpec(moved.shape, lambda i: (0, 0, 0)),
            pl.BlockSpec((BLOCK, width), lambda i: (jnp.minimum(i, blocks - 1), 0)),
        ],
        out_specs=[
            pl.BlockSpec((BLOCK, width), lambda i: (blocks + jnp.minimum(i, blocks - 1), 0)),
            pl.BlockSpec((width // LANES, onsets, LANES), lambda i: (0, 0, 0)),
        ],
        out_shape=[
            pltpu.HBM((count, width), jnp.bfloat16),
            jax.ShapeDtypeStruct((width // LANES, onsets, LANES), jnp.float32),
        ],
        scratch_shapes=[
            pltpu.VMEM((4, BLOCK, LANES), jnp.float32),
            pltpu.VMEM((48, width), jnp.bfloat16),
            pltpu.VMEM((32, 4 * LANES), jnp.bfloat16),
            pltpu.VMEM((BLOCK, width), jnp.bfloat16),
            pltpu.VMEM((BLOCK, width), jnp.bfloat16),
        ],
        input_output_aliases={3: 0},
        compiler_params=pltpu.CompilerParams(vmem_limit_bytes=FINISH_BYTES),
        name="finish",
    )(factors, targets, moved, tile)


def apply_kernel(moved_ref, tile_ref, product_ref):
    step = pl.program_id(0)
    chunks = range(tile_ref.shape[1] // LANES)
    part = jnp.concatenate([moved_ref[i] for i in range(moved_ref.shape[0])], axis=1)
    product = jnp.dot(part, tile_ref[...], preferred_element_type=jnp.float32)

    @pl.when(step == 0)
    def _():
        for chunk in chunks:
            product_ref[chunk] = product[:, chunk * LANES : (chunk + 1) * LANES]

    @pl.when(step > 0)
    def _():
        for chunk in chunks:
            product_ref[chunk] += product[:, chunk * LANES : (chunk + 1) * LANES]


def apply(moved, tile, depth=1024):
    count, width = tile.shape
    onsets = moved.shape[1]
    return pl.pallas_call(
        apply_kernel,
        grid=(count // depth,),
        in_specs=[
            pl.BlockSpec((depth // LANES, onsets, LANES), lambda i: (i, 0, 0)),
            pl.BlockSpec((depth, width), lambda i: (i, 0)),
        ],
        out_specs=pl.BlockSpec((width // LANES, onsets, LANES), lambda i: (0, 0, 0)),
        out_shape=jax.ShapeDtypeStruct((width // LANES, onsets, LANES), jnp.float32),
        compiler_params=pltpu.CompilerParams(vmem_limit_bytes=VMEM_BYTES),
        name="apply",
    )(moved, tile)


def residual_kernel(part_ref, base_ref, residual_ref, sent_ref):
    residual = base_ref[...] - jnp.sum(part_ref[...], axis=0)
    residual_ref[...] = residual
    sent = residual.astype(jnp.bfloat16)
    for device in range(sent_ref.shape[0]):
        sent_ref[device] = sent


def residual_of(parts, base, devices):
    return pl.pallas_call(
        residual_kernel,
        in_specs=[WHOLE] * 2,
        out_specs=[WHOLE] * 2,
        out_shape=[
            jax.ShapeDtypeStruct(base.shape, jnp.float32),
            jax.ShapeDtypeStruct((devices,) + base.shape, jnp.bfloat16),
        ],
        compiler_params=pltpu.CompilerParams(vmem_limit_bytes=SMALL_BYTES),
        name="residual",
    )(parts, base)


def sums_kernel(part_ref, start_ref, residual_ref, center_ref, area_ref, field_ref, sent_ref):
    change = jnp.sum(part_ref[...], axis=0)
    residual = residual_ref[...]
    count = residual.shape[0]
    field_ref[:count] = start_ref[...]
    field_ref[count : 2 * count] = residual
    field_ref[2 * count : 3 * count] = change
    field_ref[3 * count :] = center_ref[...]
    area = jnp.broadcast_to(area_ref[...], residual.shape)
    weighted = area * residual
    terms = [weighted * residual, weighted * change, area * change * change, area]
    total = jnp.sum(jnp.concatenate(terms, axis=0).T, axis=0, keepdims=True)
    sent = jnp.broadcast_to(total, sent_ref.shape[1:])
    for device in range(sent_ref.shape[0]):
        sent_ref[device] = sent


def sums_of(parts, start, residual, centers, areas, devices):
    count, own = start.shape
    return pl.pallas_call(
        sums_kernel,
        in_specs=[WHOLE] * 5,
        out_specs=[WHOLE] * 2,
        out_shape=[
            jax.ShapeDtypeStruct((3 * count + 8, own), jnp.float32),
            jax.ShapeDtypeStruct((devices, 8, 4 * count), jnp.float32),
        ],
        compiler_params=pltpu.CompilerParams(vmem_limit_bytes=SMALL_BYTES),
        name="sums",
    )(parts, start, residual, centers, areas)


def regroup_kernel(part_ref, sent_ref):
    sent = jnp.sum(part_ref[...], axis=0)
    for device in range(sent_ref.shape[0]):
        sent_ref[device] = sent


def regroup(parts, devices):
    return pl.pallas_call(
        regroup_kernel,
        in_specs=[WHOLE],
        out_specs=WHOLE,
        out_shape=jax.ShapeDtypeStruct((devices,) + parts.shape[1:], jnp.float32),
        compiler_params=pltpu.CompilerParams(vmem_limit_bytes=SMALL_BYTES),
        name="regroup",
    )(parts)


def last_kernel(
    part_ref, field_ref, before_ref, after_ref, onset_ref, end_ref, state_ref, pressure_ref
):
    count, own = state_ref.shape
    total = jnp.sum(part_ref[...], axis=0)[0:1, :]
    total = jnp.broadcast_to(total, (4 * count, own)).T
    both, mixed, changed, area = (total[i * count : (i + 1) * count] for i in range(4))
    reach = CAP * jnp.sqrt(area)

    def damp(sums):
        return OMEGA * jnp.minimum(1.0, reach * lax.rsqrt(sums + EPS))

    one = damp(both)
    keep = 1.0 - 0.5 * one
    sums = keep * keep * both - 2.0 * keep * one * mixed + one * one * changed
    two = damp(jnp.maximum(sums, 0.0))
    on_residual = one + two * keep
    on_change = two * one

    def strengths(ref):
        value = ref[:count] + on_residual * ref[count : 2 * count]
        return value - on_change * ref[2 * count : 3 * count]

    state = strengths(field_ref)
    state_ref[...] = state

    def differences(middle, low, high):
        lane = lax.broadcasted_iota(jnp.int32, middle.shape, 1)
        is_first = jnp.broadcast_to(end_ref[0], middle.shape) == 1
        is_last = jnp.broadcast_to(end_ref[1], middle.shape) == 1
        low = jnp.where(is_first, middle, pltpu.roll(low, PB, 1))
        high = jnp.where(is_last, middle, pltpu.roll(high, own - PB, 1))
        lower = jnp.where(lane < PB, low, pltpu.roll(middle, PB, 1))
        upper = jnp.where(lane >= own - PB, high, pltpu.roll(middle, own - PB, 1))
        around = lane % PB
        following = jnp.where(
            around == PB - 1, pltpu.roll(middle, PB - 1, 1), pltpu.roll(middle, own - 1, 1)
        )
        preceding = jnp.where(
            around == 0, pltpu.roll(middle, own - PB + 1, 1), pltpu.roll(middle, 1, 1)
        )
        return upper - lower, following - preceding

    steps = differences(field_ref[3 * count :], before_ref[3 * count :], after_ref[3 * count :])
    changes = differences(state, strengths(before_ref), strengths(after_ref))
    pressure = jnp.ones_like(state)
    for step, change in zip(steps, changes):
        span = jnp.sqrt(jnp.sum(step * step, axis=0, keepdims=True))
        along = onset_ref[:, 0:1] * step[0:1]
        along += onset_ref[:, 1:2] * step[1:2]
        along += onset_ref[:, 2:3] * step[2:3]
        speed = along / span - change / span
        pressure -= speed * speed
    pressure_ref[...] = pressure


def last(parts, fields, before, after, onset, ends, count):
    own = fields.shape[1]
    return pl.pallas_call(
        last_kernel,
        in_specs=[WHOLE] * 5 + [pl.BlockSpec(memory_space=pltpu.SMEM)],
        out_specs=[WHOLE] * 2,
        out_shape=[jax.ShapeDtypeStruct((count, own), jnp.float32)] * 2,
        compiler_params=pltpu.CompilerParams(vmem_limit_bytes=SMALL_BYTES),
        name="last",
    )(parts, fields, before, after, onset, ends)


WHOLE = pl.BlockSpec(memory_space=pltpu.VMEM)


def per_device(centers, normals, areas, onset, start):
    row_count = lax.axis_size("row")
    col_count = lax.axis_size("col")
    row_index = lax.axis_index("row")
    col_index = lax.axis_index("col")
    own = start.shape[1]
    count = start.shape[0]
    own_first = col_index * own
    own_areas = lax.dynamic_slice_in_dim(areas, own_first, own, 0)
    own_normals = lax.dynamic_slice_in_dim(normals, own_first, own, 1)
    own_centers = lax.dynamic_slice_in_dim(centers, own_first, own, 1)

    mark = jnp.concatenate([jnp.ones((1, own)), jnp.zeros((4, own))], axis=0)
    note = jnp.concatenate([own_centers, mark.astype(jnp.float32)], axis=0)
    notes = spread(note, "row", row_count)
    factors, shown = source_factors(centers, normals, areas, start, col_count)
    right = -jnp.sum(onset[:, :, None] * own_normals[:, None, :], axis=0)
    base = right - 0.5 * start
    notes, shown, factors, base = lax.optimization_barrier((notes, shown, factors, base))
    targets = jnp.transpose(notes, (1, 0, 2)).reshape(8, row_count * own)
    moved = lax.all_to_all(shown, "col", 0, 0, tiled=True)

    tile = build(factors, targets)
    tile, partial = finish_build(factors, targets, moved, tile)

    parts = lax.all_to_all(partial, "row", 0, 0, tiled=True)
    residual, sent = residual_of(parts, base, col_count)
    gathered = lax.all_to_all(sent, "col", 0, 0, tiled=True)
    partial = apply(gathered, tile)
    parts = lax.all_to_all(partial, "row", 0, 0, tiled=True)
    here = jnp.pad(own_centers, ((0, 5), (0, 0)))
    fields, sent = sums_of(parts, start, residual, here, own_areas[None, :], col_count)

    flat = row_index * col_count + col_index
    devices = row_count * col_count
    forward = [(i, i + 1) for i in range(devices - 1)]
    backward = [(i + 1, i) for i in range(devices - 1)]
    parts = lax.all_to_all(sent, "col", 0, 0, tiled=True)
    before = lax.ppermute(fields, ("row", "col"), forward)
    parts, before, later = lax.optimization_barrier((parts, before, fields))
    after = lax.ppermute(later, ("row", "col"), backward)
    parts = lax.all_to_all(regroup(parts, row_count), "row", 0, 0, tiled=True)
    ends = jnp.stack([flat == 0, flat == devices - 1]).astype(jnp.int32)
    return last(parts, fields, before, after, onset.T, ends, count)


def solution(mesh):
    return jax.shard_map(
        per_device,
        mesh=mesh,
        in_specs=(P(None, "row"), P(None, "row"), P("row"), P(), P(None, ("row", "col"))),
        out_specs=(P(None, ("row", "col")), P(None, ("row", "col"))),
        check_vma=False,
    )
```

```python
import math

import jax
import jax.numpy as jnp
from jax import lax
from jax.experimental import pallas as pl
from jax.experimental.pallas import tpu as pltpu
from jax.sharding import PartitionSpec as P

PB = 32
SWEEPS = 2


INV_FOUR_PI = 1.0 / (4.0 * math.pi)
CAP = 0.4
OMEGA = 1.5
EPS = 1e-06
LANES = 128
STEP = 256
BLOCK = 512
VMEM_BYTES = 58 << 20
FINISH_BYTES = 50 << 20
SMALL_BYTES = 4 << 20


def spread(block, axis, count):
    copies = jnp.broadcast_to(block[None], (count,) + block.shape)
    return lax.all_to_all(copies, axis, 0, 0, tiled=True)


def three(value):
    high = value.astype(jnp.bfloat16).astype(jnp.float32)
    rest = value - high
    middle = rest.astype(jnp.bfloat16).astype(jnp.float32)
    return high, middle, rest - middle


def factor_kernel(center_ref, normal_ref, area_ref, start_ref, factor_ref, shown_ref):
    @pl.when(pl.program_id(0) == 0)
    def _():
        shown = start_ref[...].astype(jnp.bfloat16)
        for device in range(shown_ref.shape[0]):
            shown_ref[device] = shown

    width = center_ref.shape[1]
    blank = jnp.zeros((4, width), jnp.float32)
    area = area_ref[...]
    place = jnp.concatenate([center_ref[...], area, blank], axis=0)
    scaled = normal_ref[...] * (area * INV_FOUR_PI)
    level = -jnp.sum(scaled * center_ref[...], axis=0, keepdims=True)
    high, middle, low = three(jnp.concatenate([scaled, level, blank], axis=0))
    at_level = lax.broadcasted_iota(jnp.int32, high.shape, 0) == 3
    bare = jnp.where(at_level, 0.0, high)
    bare_middle = jnp.where(at_level, 0.0, middle)
    none = jnp.zeros_like(high)
    rows = [high, bare, middle, bare, bare_middle, low, none, none]
    rows += list(three(place)) + [none] * 5
    factor_ref[...] = jnp.concatenate(rows, axis=0).T.astype(jnp.bfloat16)


def source_factors(centers, normals, areas, start, devices, block=1024):
    count = centers.shape[1]
    return pl.pallas_call(
        factor_kernel,
        grid=(count // block,),
        in_specs=[
            pl.BlockSpec((3, block), lambda i: (0, i)),
            pl.BlockSpec((3, block), lambda i: (0, i)),
            pl.BlockSpec((1, block), lambda i: (0, i)),
            pl.BlockSpec(start.shape, lambda i: (0, 0)),
        ],
        out_specs=[
            pl.BlockSpec((block, LANES), lambda i: (i, 0)),
            pl.BlockSpec((devices,) + start.shape, lambda i: (0, 0, 0)),
        ],
        out_shape=[
            jax.ShapeDtypeStruct((count, LANES), jnp.bfloat16),
            jax.ShapeDtypeStruct((devices,) + start.shape, jnp.bfloat16),
        ],
        cost_estimate=pl.CostEstimate(
            flops=count * 400, bytes_accessed=count * 400, transcendentals=0
        ),
        name="factors",
    )(centers, normals, areas[None, :], start)


def target_factors(targets):
    targets = jnp.concatenate([targets, jnp.zeros_like(targets)], axis=0)
    high = targets.astype(jnp.bfloat16).astype(jnp.float32)
    rest = targets - high
    middle = rest.astype(jnp.bfloat16).astype(jnp.float32)
    low = rest - middle
    rows = [high, middle, high, low, middle, high]
    return jnp.concatenate(rows, axis=0).astype(jnp.bfloat16)


def fill(factor_ref, target_ref, wide_ref, pair_ref, column, stores):
    facing = jnp.dot(
        factor_ref[:, :48],
        pair_ref[:, column : column + STEP],
        preferred_element_type=jnp.float32,
    )
    for lane in range(0, STEP, LANES):
        here = slice(column + lane, column + lane + LANES)
        x, y, z = (target_ref[d : d + 1, here] for d in range(3))
        for row in range(0, BLOCK, 16):
            at = slice(row, row + 16)
            delta_x = x - wide_ref[0, at, :]
            delta_y = y - wide_ref[1, at, :]
            delta_z = z - wide_ref[2, at, :]
            dist_sq = delta_x * delta_x + delta_y * delta_y + delta_z * delta_z + wide_ref[3, at, :]
            inverse = lax.rsqrt(dist_sq)
            value = facing[row : row + 16, lane : lane + LANES] * (inverse * inverse * inverse)
            value = value.astype(jnp.bfloat16)
            for store in stores:
                store[at, here] = value


def prepare(target_ref, pair_ref, spread_ref):
    pair_ref[...] = target_factors(target_ref[...])
    which = lax.broadcasted_iota(jnp.int32, spread_ref.shape, 0)
    lane = lax.broadcasted_iota(jnp.int32, spread_ref.shape, 1)
    chosen = which % 8 == lane // LANES
    spread_ref[...] = jnp.where(chosen, 1.0, 0.0).astype(jnp.bfloat16)


def spread_params(factor_ref, spread_ref, wide_ref):
    wide = jnp.dot(factor_ref[:, 64:96], spread_ref[...], preferred_element_type=jnp.float32)
    for row in range(4):
        wide_ref[row] = wide[:, row * LANES : (row + 1) * LANES]


def build_kernel(factor_ref, target_ref, tile_ref, wide_ref, pair_ref, spread_ref):
    @pl.when(pl.program_id(0) == 0)
    def _():
        prepare(target_ref, pair_ref, spread_ref)

    spread_params(factor_ref, spread_ref, wide_ref)
    for column in range(0, tile_ref.shape[1], STEP):
        fill(factor_ref, target_ref, wide_ref, pair_ref, column, [tile_ref])


def finish_kernel(
    factor_ref,
    target_ref,
    moved_ref,
    old_ref,
    tile_ref,
    product_ref,
    wide_ref,
    pair_ref,
    spread_ref,
    even_ref,
    odd_ref,
):
    step = pl.program_id(0)
    blocks = pl.num_programs(0) - 1
    width = tile_ref.shape[1]
    deep = BLOCK // LANES

    @pl.when(step == 0)
    def _():
        prepare(target_ref, pair_ref, spread_ref)
        product_ref[...] = jnp.zeros_like(product_ref)

    def dot(block, ref, column):
        part = jnp.concatenate([moved_ref[deep * block + i] for i in range(deep)], axis=1)
        return jnp.dot(
            part, ref[:, column : column + STEP], preferred_element_type=jnp.float32
        )

    def add_to(column, value):
        for lane in range(0, STEP, LANES):
            product_ref[(column + lane) // LANES] += value[:, lane : lane + LANES]

    def whole(now_ref, before_ref):
        spread_params(factor_ref, spread_ref, wide_ref)
        for column in range(0, width, STEP):
            value = dot(step, old_ref, column)
            if before_ref is not None:
                value += dot(blocks + step - 1, before_ref, column)
            fill(
                factor_ref, target_ref, wide_ref, pair_ref, column, [tile_ref, now_ref]
            )
            add_to(column, value)

    @pl.when(step == 0)
    def _():
        whole(even_ref, None)

    @pl.when((step > 0) & (step < blocks) & (step % 2 == 0))
    def _():
        whole(even_ref, odd_ref)

    @pl.when((step < blocks) & (step % 2 == 1))
    def _():
        whole(odd_ref, even_ref)

    @pl.when((step == blocks) & (step % 2 == 0))
    def _():
        for column in range(0, width, STEP):
            add_to(column, dot(blocks + step - 1, odd_ref, column))

    @pl.when((step == blocks) & (step % 2 == 1))
    def _():
        for column in range(0, width, STEP):
            add_to(column, dot(blocks + step - 1, even_ref, column))


def build(factors, targets):
    count = factors.shape[0]
    width = targets.shape[1]
    return pl.pallas_call(
        build_kernel,
        grid=(count // BLOCK // 2,),
        in_specs=[
            pl.BlockSpec((BLOCK, LANES), lambda i: (i, 0)),
            pl.BlockSpec((4, width), lambda i: (0, 0)),
        ],
        out_specs=pl.BlockSpec((BLOCK, width), lambda i: (i, 0)),
        out_shape=pltpu.HBM((count, width), jnp.bfloat16),
        scratch_shapes=[
            pltpu.VMEM((4, BLOCK, LANES), jnp.float32),
            pltpu.VMEM((48, width), jnp.bfloat16),
            pltpu.VMEM((32, 4 * LANES), jnp.bfloat16),
        ],
        compiler_params=pltpu.CompilerParams(vmem_limit_bytes=VMEM_BYTES),
        cost_estimate=pl.CostEstimate(
            flops=count * width * 50, bytes_accessed=count * width, transcendentals=count * width // 2
        ),
        name="build",
    )(factors, targets)


def finish_build(factors, targets, moved, tile):
    count, width = tile.shape
    blocks = count // BLOCK // 2
    onsets = moved.shape[1]
    return pl.pallas_call(
        finish_kernel,
        grid=(blocks + 1,),
        in_specs=[
            pl.BlockSpec((BLOCK, LANES), lambda i: (blocks + jnp.minimum(i, blocks - 1), 0)),
            pl.BlockSpec((4, width), lambda i: (0, 0)),
            pl.BlockSpec(moved.shape, lambda i: (0, 0, 0)),
            pl.BlockSpec((BLOCK, width), lambda i: (jnp.minimum(i, blocks - 1), 0)),
        ],
        out_specs=[
            pl.BlockSpec((BLOCK, width), lambda i: (blocks + jnp.minimum(i, blocks - 1), 0)),
            pl.BlockSpec((width // LANES, onsets, LANES), lambda i: (0, 0, 0)),
        ],
        out_shape=[
            pltpu.HBM((count, width), jnp.bfloat16),
            jax.ShapeDtypeStruct((width // LANES, onsets, LANES), jnp.float32),
        ],
        scratch_shapes=[
            pltpu.VMEM((4, BLOCK, LANES), jnp.float32),
            pltpu.VMEM((48, width), jnp.bfloat16),
            pltpu.VMEM((32, 4 * LANES), jnp.bfloat16),
            pltpu.VMEM((BLOCK, width), jnp.bfloat16),
            pltpu.VMEM((BLOCK, width), jnp.bfloat16),
        ],
        input_output_aliases={3: 0},
        compiler_params=pltpu.CompilerParams(vmem_limit_bytes=FINISH_BYTES),
        name="finish",
    )(factors, targets, moved, tile)


def apply_kernel(moved_ref, tile_ref, product_ref):
    step = pl.program_id(0)
    chunks = range(tile_ref.shape[1] // LANES)
    part = jnp.concatenate([moved_ref[i] for i in range(moved_ref.shape[0])], axis=1)
    product = jnp.dot(part, tile_ref[...], preferred_element_type=jnp.float32)

    @pl.when(step == 0)
    def _():
        for chunk in chunks:
            product_ref[chunk] = product[:, chunk * LANES : (chunk + 1) * LANES]

    @pl.when(step > 0)
    def _():
        for chunk in chunks:
            product_ref[chunk] += product[:, chunk * LANES : (chunk + 1) * LANES]


def apply(moved, tile, depth=1024):
    count, width = tile.shape
    onsets = moved.shape[1]
    return pl.pallas_call(
        apply_kernel,
        grid=(count // depth,),
        in_specs=[
            pl.BlockSpec((depth // LANES, onsets, LANES), lambda i: (i, 0, 0)),
            pl.BlockSpec((depth, width), lambda i: (i, 0)),
        ],
        out_specs=pl.BlockSpec((width // LANES, onsets, LANES), lambda i: (0, 0, 0)),
        out_shape=jax.ShapeDtypeStruct((width // LANES, onsets, LANES), jnp.float32),
        compiler_params=pltpu.CompilerParams(vmem_limit_bytes=VMEM_BYTES),
        name="apply",
    )(moved, tile)


def residual_kernel(part_ref, base_ref, residual_ref, sent_ref):
    residual = base_ref[...] - jnp.sum(part_ref[...], axis=0)
    residual_ref[...] = residual
    sent = residual.astype(jnp.bfloat16)
    for device in range(sent_ref.shape[0]):
        sent_ref[device] = sent


def residual_of(parts, base, devices):
    return pl.pallas_call(
        residual_kernel,
        in_specs=[WHOLE] * 2,
        out_specs=[WHOLE] * 2,
        out_shape=[
            jax.ShapeDtypeStruct(base.shape, jnp.float32),
            jax.ShapeDtypeStruct((devices,) + base.shape, jnp.bfloat16),
        ],
        compiler_params=pltpu.CompilerParams(vmem_limit_bytes=SMALL_BYTES),
        name="residual",
    )(parts, base)


def sums_kernel(part_ref, start_ref, residual_ref, center_ref, area_ref, field_ref, sent_ref):
    change = jnp.sum(part_ref[...], axis=0)
    residual = residual_ref[...]
    count = residual.shape[0]
    field_ref[:count] = start_ref[...]
    field_ref[count : 2 * count] = residual
    field_ref[2 * count : 3 * count] = change
    field_ref[3 * count :] = center_ref[...]
    area = jnp.broadcast_to(area_ref[...], residual.shape)
    weighted = area * residual
    terms = [weighted * residual, weighted * change, area * change * change, area]
    total = jnp.sum(jnp.concatenate(terms, axis=0).T, axis=0, keepdims=True)
    for device in range(sent_ref.shape[0]):
        sent_ref[device] = jnp.broadcast_to(total, sent_ref.shape[1:])


def sums_of(parts, start, residual, centers, areas, devices):
    count, own = start.shape
    return pl.pallas_call(
        sums_kernel,
        in_specs=[WHOLE] * 5,
        out_specs=[WHOLE] * 2,
        out_shape=[
            jax.ShapeDtypeStruct((3 * count + 8, own), jnp.float32),
            jax.ShapeDtypeStruct((devices, 2, 4 * count), jnp.float32),
        ],
        compiler_params=pltpu.CompilerParams(vmem_limit_bytes=SMALL_BYTES),
        name="sums",
    )(parts, start, residual, centers, areas)


def regroup_kernel(part_ref, sent_ref):
    sent = jnp.broadcast_to(jnp.sum(part_ref[...], axis=0)[0:1, :], sent_ref.shape[1:])
    for device in range(sent_ref.shape[0]):
        sent_ref[device] = sent


def regroup(parts, devices):
    return pl.pallas_call(
        regroup_kernel,
        in_specs=[WHOLE],
        out_specs=WHOLE,
        out_shape=jax.ShapeDtypeStruct((devices, 8, parts.shape[2]), jnp.float32),
        compiler_params=pltpu.CompilerParams(vmem_limit_bytes=SMALL_BYTES),
        name="regroup",
    )(parts)


def last_kernel(
    part_ref, field_ref, before_ref, after_ref, onset_ref, end_ref, state_ref, pressure_ref
):
    count, own = state_ref.shape
    total = jnp.sum(part_ref[...], axis=0)[0:1, :]
    total = jnp.broadcast_to(total, (4 * count, own)).T
    both, mixed, changed, area = (total[i * count : (i + 1) * count] for i in range(4))
    reach = CAP * jnp.sqrt(area)

    def damp(sums):
        return OMEGA * jnp.minimum(1.0, reach * lax.rsqrt(sums + EPS))

    one = damp(both)
    keep = 1.0 - 0.5 * one
    sums = keep * keep * both - 2.0 * keep * one * mixed + one * one * changed
    two = damp(jnp.maximum(sums, 0.0))
    on_residual = one + two * keep
    on_change = two * one

    def strengths(ref):
        value = ref[:count] + on_residual * ref[count : 2 * count]
        return value - on_change * ref[2 * count : 3 * count]

    state = strengths(field_ref)
    state_ref[...] = state

    def differences(middle, low, high):
        lane = lax.broadcasted_iota(jnp.int32, middle.shape, 1)
        is_first = jnp.broadcast_to(end_ref[0], middle.shape) == 1
        is_last = jnp.broadcast_to(end_ref[1], middle.shape) == 1
        low = jnp.where(is_first, middle, pltpu.roll(low, PB, 1))
        high = jnp.where(is_last, middle, pltpu.roll(high, own - PB, 1))
        lower = jnp.where(lane < PB, low, pltpu.roll(middle, PB, 1))
        upper = jnp.where(lane >= own - PB, high, pltpu.roll(middle, own - PB, 1))
        around = lane % PB
        following = jnp.where(
            around == PB - 1, pltpu.roll(middle, PB - 1, 1), pltpu.roll(middle, own - 1, 1)
        )
        preceding = jnp.where(
            around == 0, pltpu.roll(middle, own - PB + 1, 1), pltpu.roll(middle, 1, 1)
        )
        return upper - lower, following - preceding

    steps = differences(field_ref[3 * count :], before_ref[3 * count :], after_ref[3 * count :])
    changes = differences(state, strengths(before_ref), strengths(after_ref))
    pressure = jnp.ones_like(state)
    for step, change in zip(steps, changes):
        span = jnp.sqrt(jnp.sum(step * step, axis=0, keepdims=True))
        along = onset_ref[:, 0:1] * step[0:1]
        along += onset_ref[:, 1:2] * step[1:2]
        along += onset_ref[:, 2:3] * step[2:3]
        speed = along / span - change / span
        pressure -= speed * speed
    pressure_ref[...] = pressure


def last(parts, fields, before, after, onset, ends, count):
    own = fields.shape[1]
    return pl.pallas_call(
        last_kernel,
        in_specs=[WHOLE] * 5 + [pl.BlockSpec(memory_space=pltpu.SMEM)],
        out_specs=[WHOLE] * 2,
        out_shape=[jax.ShapeDtypeStruct((count, own), jnp.float32)] * 2,
        compiler_params=pltpu.CompilerParams(vmem_limit_bytes=SMALL_BYTES),
        name="last",
    )(parts, fields, before, after, onset, ends)


WHOLE = pl.BlockSpec(memory_space=pltpu.VMEM)


def per_device(centers, normals, areas, onset, start):
    row_count = lax.axis_size("row")
    col_count = lax.axis_size("col")
    row_index = lax.axis_index("row")
    col_index = lax.axis_index("col")
    own = start.shape[1]
    count = start.shape[0]
    own_first = col_index * own
    own_areas = lax.dynamic_slice_in_dim(areas, own_first, own, 0)
    own_normals = lax.dynamic_slice_in_dim(normals, own_first, own, 1)
    own_centers = lax.dynamic_slice_in_dim(centers, own_first, own, 1)

    note = jnp.concatenate([own_centers, jnp.ones((1, own), jnp.float32)], axis=0)
    notes = spread(note, "row", row_count)
    factors, shown = source_factors(centers, normals, areas, start, col_count)
    right = -jnp.sum(onset[:, :, None] * own_normals[:, None, :], axis=0)
    base = right - 0.5 * start
    notes, shown, factors, base = lax.optimization_barrier((notes, shown, factors, base))
    targets = jnp.transpose(notes, (1, 0, 2)).reshape(4, row_count * own)
    moved = lax.all_to_all(shown, "col", 0, 0, tiled=True)

    tile = build(factors, targets)
    tile, partial = finish_build(factors, targets, moved, tile)

    parts = lax.all_to_all(partial, "row", 0, 0, tiled=True)
    residual, sent = residual_of(parts, base, col_count)
    gathered = lax.all_to_all(sent, "col", 0, 0, tiled=True)
    partial = apply(gathered, tile)
    parts = lax.all_to_all(partial, "row", 0, 0, tiled=True)
    here = jnp.pad(own_centers, ((0, 5), (0, 0)))
    fields, sent = sums_of(parts, start, residual, here, own_areas[None, :], col_count)

    flat = row_index * col_count + col_index
    devices = row_count * col_count
    forward = [(i, i + 1) for i in range(devices - 1)]
    backward = [(i + 1, i) for i in range(devices - 1)]
    parts = lax.all_to_all(sent, "col", 0, 0, tiled=True)
    before = lax.ppermute(fields, ("row", "col"), forward)
    sent, before, later = lax.optimization_barrier((regroup(parts, row_count), before, fields))
    after = lax.ppermute(later, ("row", "col"), backward)
    parts = lax.all_to_all(sent, "row", 0, 0, tiled=True)
    ends = jnp.stack([flat == 0, flat == devices - 1]).astype(jnp.int32)
    return last(parts, fields, before, after, onset.T, ends, count)


def solution(mesh):
    return jax.shard_map(
        per_device,
        mesh=mesh,
        in_specs=(P(None, "row"), P(None, "row"), P("row"), P(), P(None, ("row", "col"))),
        out_specs=(P(None, ("row", "col")), P(None, ("row", "col"))),
        check_vma=False,
    )
```

```python
import math

import jax
import jax.numpy as jnp
from jax import lax
from jax.experimental import pallas as pl
from jax.experimental.pallas import tpu as pltpu
from jax.sharding import PartitionSpec as P

PB = 32
SWEEPS = 2


INV_FOUR_PI = 1.0 / (4.0 * math.pi)
CAP = 0.4
OMEGA = 1.5
EPS = 1e-06
LANES = 128
STEP = 256
BLOCK = 512
VMEM_BYTES = 58 << 20
FINISH_BYTES = 50 << 20
SMALL_BYTES = 4 << 20


def spread(block, axis, count):
    copies = jnp.broadcast_to(block[None], (count,) + block.shape)
    return lax.all_to_all(copies, axis, 0, 0, tiled=True)


def three(value):
    high = value.astype(jnp.bfloat16).astype(jnp.float32)
    rest = value - high
    middle = rest.astype(jnp.bfloat16).astype(jnp.float32)
    return high, middle, rest - middle


def factor_kernel(center_ref, normal_ref, area_ref, start_ref, factor_ref, shown_ref):
    @pl.when(pl.program_id(0) == 0)
    def _():
        shown = start_ref[...].astype(jnp.bfloat16)
        for device in range(shown_ref.shape[0]):
            shown_ref[device] = shown

    width = center_ref.shape[1]
    blank = jnp.zeros((4, width), jnp.float32)
    area = area_ref[...]
    place = jnp.concatenate([center_ref[...], area, blank], axis=0)
    scaled = normal_ref[...] * (area * INV_FOUR_PI)
    level = -jnp.sum(scaled * center_ref[...], axis=0, keepdims=True)
    high, middle, low = three(jnp.concatenate([scaled, level, blank], axis=0))
    at_level = lax.broadcasted_iota(jnp.int32, high.shape, 0) == 3
    bare = jnp.where(at_level, 0.0, high)
    bare_middle = jnp.where(at_level, 0.0, middle)
    none = jnp.zeros_like(high)
    rows = [high, bare, middle, bare, bare_middle, low, none, none]
    rows += list(three(place)) + [none] * 5
    factor_ref[...] = jnp.concatenate(rows, axis=0).T.astype(jnp.bfloat16)


def source_factors(centers, normals, areas, start, devices, block=1024):
    count = centers.shape[1]
    return pl.pallas_call(
        factor_kernel,
        grid=(count // block,),
        in_specs=[
            pl.BlockSpec((3, block), lambda i: (0, i)),
            pl.BlockSpec((3, block), lambda i: (0, i)),
            pl.BlockSpec((1, block), lambda i: (0, i)),
            pl.BlockSpec(start.shape, lambda i: (0, 0)),
        ],
        out_specs=[
            pl.BlockSpec((block, LANES), lambda i: (i, 0)),
            pl.BlockSpec((devices,) + start.shape, lambda i: (0, 0, 0)),
        ],
        out_shape=[
            jax.ShapeDtypeStruct((count, LANES), jnp.bfloat16),
            jax.ShapeDtypeStruct((devices,) + start.shape, jnp.bfloat16),
        ],
        cost_estimate=pl.CostEstimate(
            flops=count * 400, bytes_accessed=count * 400, transcendentals=0
        ),
        name="factors",
    )(centers, normals, areas[None, :], start)


def target_factors(targets):
    targets = jnp.concatenate([targets, jnp.zeros_like(targets)], axis=0)
    high = targets.astype(jnp.bfloat16).astype(jnp.float32)
    rest = targets - high
    middle = rest.astype(jnp.bfloat16).astype(jnp.float32)
    low = rest - middle
    rows = [high, middle, high, low, middle, high]
    return jnp.concatenate(rows, axis=0).astype(jnp.bfloat16)


def fill(factor_ref, target_ref, wide_ref, pair_ref, column, stores):
    facing = jnp.dot(
        factor_ref[:, :48],
        pair_ref[:, column : column + STEP],
        preferred_element_type=jnp.float32,
    )
    for lane in range(0, STEP, LANES):
        here = slice(column + lane, column + lane + LANES)
        x, y, z = (target_ref[d : d + 1, here] for d in range(3))
        for row in range(0, BLOCK, 16):
            at = slice(row, row + 16)
            delta_x = x - wide_ref[0, at, :]
            delta_y = y - wide_ref[1, at, :]
            delta_z = z - wide_ref[2, at, :]
            dist_sq = delta_x * delta_x + delta_y * delta_y + delta_z * delta_z + wide_ref[3, at, :]
            inverse = lax.rsqrt(dist_sq)
            value = facing[row : row + 16, lane : lane + LANES] * (inverse * inverse * inverse)
            value = value.astype(jnp.bfloat16)
            for store in stores:
                store[at, here] = value


def prepare(target_ref, pair_ref, spread_ref):
    pair_ref[...] = target_factors(target_ref[...])
    which = lax.broadcasted_iota(jnp.int32, spread_ref.shape, 0)
    lane = lax.broadcasted_iota(jnp.int32, spread_ref.shape, 1)
    chosen = which % 8 == lane // LANES
    spread_ref[...] = jnp.where(chosen, 1.0, 0.0).astype(jnp.bfloat16)


def spread_params(factor_ref, spread_ref, wide_ref):
    wide = jnp.dot(factor_ref[:, 64:96], spread_ref[...], preferred_element_type=jnp.float32)
    for row in range(4):
        wide_ref[row] = wide[:, row * LANES : (row + 1) * LANES]


def build_kernel(factor_ref, target_ref, tile_ref, wide_ref, pair_ref, spread_ref):
    @pl.when(pl.program_id(0) == 0)
    def _():
        prepare(target_ref, pair_ref, spread_ref)

    spread_params(factor_ref, spread_ref, wide_ref)
    for column in range(0, tile_ref.shape[1], STEP):
        fill(factor_ref, target_ref, wide_ref, pair_ref, column, [tile_ref])


def finish_kernel(
    factor_ref,
    target_ref,
    moved_ref,
    old_ref,
    tile_ref,
    product_ref,
    wide_ref,
    pair_ref,
    spread_ref,
    even_ref,
    odd_ref,
):
    step = pl.program_id(0)
    blocks = pl.num_programs(0) - 1
    width = tile_ref.shape[1]
    deep = BLOCK // LANES

    @pl.when(step == 0)
    def _():
        prepare(target_ref, pair_ref, spread_ref)
        product_ref[...] = jnp.zeros_like(product_ref)

    def dot(block, ref, column):
        part = jnp.concatenate([moved_ref[deep * block + i] for i in range(deep)], axis=1)
        return jnp.dot(
            part, ref[:, column : column + STEP], preferred_element_type=jnp.float32
        )

    def add_to(column, value):
        for lane in range(0, STEP, LANES):
            product_ref[(column + lane) // LANES] += value[:, lane : lane + LANES]

    def whole(now_ref, before_ref):
        spread_params(factor_ref, spread_ref, wide_ref)
        for column in range(0, width, STEP):
            value = dot(step, old_ref, column)
            if before_ref is not None:
                value += dot(blocks + step - 1, before_ref, column)
            fill(
                factor_ref, target_ref, wide_ref, pair_ref, column, [tile_ref, now_ref]
            )
            add_to(column, value)

    @pl.when(step == 0)
    def _():
        whole(even_ref, None)

    @pl.when((step > 0) & (step < blocks) & (step % 2 == 0))
    def _():
        whole(even_ref, odd_ref)

    @pl.when((step < blocks) & (step % 2 == 1))
    def _():
        whole(odd_ref, even_ref)

    @pl.when((step == blocks) & (step % 2 == 0))
    def _():
        for column in range(0, width, STEP):
            add_to(column, dot(blocks + step - 1, odd_ref, column))

    @pl.when((step == blocks) & (step % 2 == 1))
    def _():
        for column in range(0, width, STEP):
            add_to(column, dot(blocks + step - 1, even_ref, column))


def build(factors, targets):
    count = factors.shape[0]
    width = targets.shape[1]
    return pl.pallas_call(
        build_kernel,
        grid=(count // BLOCK // 2,),
        in_specs=[
            pl.BlockSpec((BLOCK, LANES), lambda i: (i, 0)),
            pl.BlockSpec((4, width), lambda i: (0, 0)),
        ],
        out_specs=pl.BlockSpec((BLOCK, width), lambda i: (i, 0)),
        out_shape=pltpu.HBM((count, width), jnp.bfloat16),
        scratch_shapes=[
            pltpu.VMEM((4, BLOCK, LANES), jnp.float32),
            pltpu.VMEM((48, width), jnp.bfloat16),
            pltpu.VMEM((32, 4 * LANES), jnp.bfloat16),
        ],
        compiler_params=pltpu.CompilerParams(vmem_limit_bytes=VMEM_BYTES),
        cost_estimate=pl.CostEstimate(
            flops=count * width * 50, bytes_accessed=count * width, transcendentals=count * width // 2
        ),
        name="build",
    )(factors, targets)


def finish_build(factors, targets, moved, tile):
    count, width = tile.shape
    blocks = count // BLOCK // 2
    onsets = moved.shape[1]
    return pl.pallas_call(
        finish_kernel,
        grid=(blocks + 1,),
        in_specs=[
            pl.BlockSpec((BLOCK, LANES), lambda i: (blocks + jnp.minimum(i, blocks - 1), 0)),
            pl.BlockSpec((4, width), lambda i: (0, 0)),
            pl.BlockSpec(moved.shape, lambda i: (0, 0, 0)),
            pl.BlockSpec((BLOCK, width), lambda i: (jnp.minimum(i, blocks - 1), 0)),
        ],
        out_specs=[
            pl.BlockSpec((BLOCK, width), lambda i: (blocks + jnp.minimum(i, blocks - 1), 0)),
            pl.BlockSpec((width // LANES, onsets, LANES), lambda i: (0, 0, 0)),
        ],
        out_shape=[
            pltpu.HBM((count, width), jnp.bfloat16),
            jax.ShapeDtypeStruct((width // LANES, onsets, LANES), jnp.float32),
        ],
        scratch_shapes=[
            pltpu.VMEM((4, BLOCK, LANES), jnp.float32),
            pltpu.VMEM((48, width), jnp.bfloat16),
            pltpu.VMEM((32, 4 * LANES), jnp.bfloat16),
            pltpu.VMEM((BLOCK, width), jnp.bfloat16),
            pltpu.VMEM((BLOCK, width), jnp.bfloat16),
        ],
        input_output_aliases={3: 0},
        compiler_params=pltpu.CompilerParams(vmem_limit_bytes=FINISH_BYTES),
        name="finish",
    )(factors, targets, moved, tile)


def apply_kernel(moved_ref, tile_ref, product_ref):
    step = pl.program_id(0)
    chunks = range(tile_ref.shape[1] // LANES)
    part = jnp.concatenate([moved_ref[i] for i in range(moved_ref.shape[0])], axis=1)
    product = jnp.dot(part, tile_ref[...], preferred_element_type=jnp.float32)

    @pl.when(step == 0)
    def _():
        for chunk in chunks:
            product_ref[chunk] = product[:, chunk * LANES : (chunk + 1) * LANES]

    @pl.when(step > 0)
    def _():
        for chunk in chunks:
            product_ref[chunk] += product[:, chunk * LANES : (chunk + 1) * LANES]


def apply(moved, tile, depth=1024):
    count, width = tile.shape
    onsets = moved.shape[1]
    return pl.pallas_call(
        apply_kernel,
        grid=(count // depth,),
        in_specs=[
            pl.BlockSpec((depth // LANES, onsets, LANES), lambda i: (i, 0, 0)),
            pl.BlockSpec((depth, width), lambda i: (i, 0)),
        ],
        out_specs=pl.BlockSpec((width // LANES, onsets, LANES), lambda i: (0, 0, 0)),
        out_shape=jax.ShapeDtypeStruct((width // LANES, onsets, LANES), jnp.float32),
        compiler_params=pltpu.CompilerParams(vmem_limit_bytes=VMEM_BYTES),
        name="apply",
    )(moved, tile)


def residual_kernel(part_ref, base_ref, residual_ref, sent_ref):
    residual = base_ref[...] - jnp.sum(part_ref[...], axis=0)
    residual_ref[...] = residual
    sent = residual.astype(jnp.bfloat16)
    for device in range(sent_ref.shape[0]):
        sent_ref[device] = sent


def residual_of(parts, base, devices):
    return pl.pallas_call(
        residual_kernel,
        in_specs=[WHOLE] * 2,
        out_specs=[WHOLE] * 2,
        out_shape=[
            jax.ShapeDtypeStruct(base.shape, jnp.float32),
            jax.ShapeDtypeStruct((devices,) + base.shape, jnp.bfloat16),
        ],
        compiler_params=pltpu.CompilerParams(vmem_limit_bytes=SMALL_BYTES),
        name="residual",
    )(parts, base)


def sums_kernel(part_ref, start_ref, residual_ref, center_ref, area_ref, field_ref, sent_ref):
    change = jnp.sum(part_ref[...], axis=0)
    residual = residual_ref[...]
    count = residual.shape[0]
    field_ref[:count] = start_ref[...]
    field_ref[count : 2 * count] = residual
    field_ref[2 * count : 3 * count] = change
    field_ref[3 * count :] = center_ref[...]
    area = jnp.broadcast_to(area_ref[...], residual.shape)
    weighted = area * residual
    terms = [weighted * residual, weighted * change, area * change * change, area]
    total = jnp.sum(jnp.concatenate(terms, axis=0).T, axis=0, keepdims=True)
    for device in range(sent_ref.shape[0]):
        sent_ref[device] = jnp.broadcast_to(total, sent_ref.shape[1:])


def sums_of(parts, start, residual, centers, areas, devices):
    count, own = start.shape
    return pl.pallas_call(
        sums_kernel,
        in_specs=[WHOLE] * 5,
        out_specs=[WHOLE] * 2,
        out_shape=[
            jax.ShapeDtypeStruct((3 * count + 8, own), jnp.float32),
            jax.ShapeDtypeStruct((devices, 2, 4 * count), jnp.float32),
        ],
        compiler_params=pltpu.CompilerParams(vmem_limit_bytes=SMALL_BYTES),
        name="sums",
    )(parts, start, residual, centers, areas)


def regroup_kernel(part_ref, sent_ref):
    sent = jnp.broadcast_to(jnp.sum(part_ref[...], axis=0)[0:1, :], sent_ref.shape[1:])
    for device in range(sent_ref.shape[0]):
        sent_ref[device] = sent


def regroup(parts, devices):
    return pl.pallas_call(
        regroup_kernel,
        in_specs=[WHOLE],
        out_specs=WHOLE,
        out_shape=jax.ShapeDtypeStruct((devices, 8, parts.shape[2]), jnp.float32),
        compiler_params=pltpu.CompilerParams(vmem_limit_bytes=SMALL_BYTES),
        name="regroup",
    )(parts)


def last_kernel(
    part_ref, field_ref, before_ref, after_ref, onset_ref, end_ref, state_ref, pressure_ref
):
    count, own = state_ref.shape
    total = jnp.sum(part_ref[...], axis=0)[0:1, :]
    total = jnp.broadcast_to(total, (4 * count, own)).T
    both, mixed, changed, area = (total[i * count : (i + 1) * count] for i in range(4))
    reach = CAP * jnp.sqrt(area)

    def damp(sums):
        return OMEGA * jnp.minimum(1.0, reach * lax.rsqrt(sums + EPS))

    one = damp(both)
    keep = 1.0 - 0.5 * one
    sums = keep * keep * both - 2.0 * keep * one * mixed + one * one * changed
    two = damp(jnp.maximum(sums, 0.0))
    on_residual = one + two * keep
    on_change = two * one

    def strengths(ref):
        value = ref[:count] + on_residual * ref[count : 2 * count]
        return value - on_change * ref[2 * count : 3 * count]

    state = strengths(field_ref)
    state_ref[...] = state

    def differences(middle, low, high):
        lane = lax.broadcasted_iota(jnp.int32, middle.shape, 1)
        is_first = jnp.broadcast_to(end_ref[0], middle.shape) == 1
        is_last = jnp.broadcast_to(end_ref[1], middle.shape) == 1
        low = jnp.where(is_first, middle, pltpu.roll(low, PB, 1))
        high = jnp.where(is_last, middle, pltpu.roll(high, own - PB, 1))
        lower = jnp.where(lane < PB, low, pltpu.roll(middle, PB, 1))
        upper = jnp.where(lane >= own - PB, high, pltpu.roll(middle, own - PB, 1))
        around = lane % PB
        following = jnp.where(
            around == PB - 1, pltpu.roll(middle, PB - 1, 1), pltpu.roll(middle, own - 1, 1)
        )
        preceding = jnp.where(
            around == 0, pltpu.roll(middle, own - PB + 1, 1), pltpu.roll(middle, 1, 1)
        )
        return upper - lower, following - preceding

    steps = differences(field_ref[3 * count :], before_ref[3 * count :], after_ref[3 * count :])
    changes = differences(state, strengths(before_ref), strengths(after_ref))
    pressure = jnp.ones_like(state)
    for step, change in zip(steps, changes):
        span = jnp.sqrt(jnp.sum(step * step, axis=0, keepdims=True))
        along = onset_ref[:, 0:1] * step[0:1]
        along += onset_ref[:, 1:2] * step[1:2]
        along += onset_ref[:, 2:3] * step[2:3]
        speed = along / span - change / span
        pressure -= speed * speed
    pressure_ref[...] = pressure


def last(parts, fields, before, after, onset, ends, count):
    own = fields.shape[1]
    return pl.pallas_call(
        last_kernel,
        in_specs=[WHOLE] * 5 + [pl.BlockSpec(memory_space=pltpu.SMEM)],
        out_specs=[WHOLE] * 2,
        out_shape=[jax.ShapeDtypeStruct((count, own), jnp.float32)] * 2,
        compiler_params=pltpu.CompilerParams(vmem_limit_bytes=SMALL_BYTES),
        name="last",
    )(parts, fields, before, after, onset, ends)


WHOLE = pl.BlockSpec(memory_space=pltpu.VMEM)


def per_device(centers, normals, areas, onset, start):
    row_count = lax.axis_size("row")
    col_count = lax.axis_size("col")
    row_index = lax.axis_index("row")
    col_index = lax.axis_index("col")
    own = start.shape[1]
    count = start.shape[0]
    own_first = col_index * own
    own_areas = lax.dynamic_slice_in_dim(areas, own_first, own, 0)
    own_normals = lax.dynamic_slice_in_dim(normals, own_first, own, 1)
    own_centers = lax.dynamic_slice_in_dim(centers, own_first, own, 1)

    note = jnp.concatenate([own_centers, jnp.ones((1, own), jnp.float32)], axis=0)
    notes = spread(note, "row", row_count)
    factors, shown = source_factors(centers, normals, areas, start, col_count)
    right = -jnp.sum(onset[:, :, None] * own_normals[:, None, :], axis=0)
    base = right - 0.5 * start
    notes, shown, factors, base = lax.optimization_barrier((notes, shown, factors, base))
    targets = jnp.transpose(notes, (1, 0, 2)).reshape(4, row_count * own)
    moved = lax.all_to_all(shown, "col", 0, 0, tiled=True)

    targets = pltpu.with_memory_space_constraint(targets, pltpu.HBM)
    tile = build(factors, targets)
    tile, partial = finish_build(factors, targets, moved, tile)

    parts = lax.all_to_all(partial, "row", 0, 0, tiled=True)
    residual, sent = residual_of(parts, base, col_count)
    gathered = lax.all_to_all(sent, "col", 0, 0, tiled=True)
    partial = apply(gathered, tile)
    parts = lax.all_to_all(partial, "row", 0, 0, tiled=True)
    here = jnp.pad(own_centers, ((0, 5), (0, 0)))
    fields, sent = sums_of(parts, start, residual, here, own_areas[None, :], col_count)

    flat = row_index * col_count + col_index
    devices = row_count * col_count
    forward = [(i, i + 1) for i in range(devices - 1)]
    backward = [(i + 1, i) for i in range(devices - 1)]
    parts = lax.all_to_all(sent, "col", 0, 0, tiled=True)
    before = lax.ppermute(fields, ("row", "col"), forward)
    sent, before, later = lax.optimization_barrier((regroup(parts, row_count), before, fields))
    after = lax.ppermute(later, ("row", "col"), backward)
    parts = lax.all_to_all(sent, "row", 0, 0, tiled=True)
    ends = jnp.stack([flat == 0, flat == devices - 1]).astype(jnp.int32)
    return last(parts, fields, before, after, onset.T, ends, count)


def solution(mesh):
    return jax.shard_map(
        per_device,
        mesh=mesh,
        in_specs=(P(None, "row"), P(None, "row"), P("row"), P(), P(None, ("row", "col"))),
        out_specs=(P(None, ("row", "col")), P(None, ("row", "col"))),
        check_vma=False,
    )
```

```python
import math

import jax
import jax.numpy as jnp
from jax import lax
from jax.experimental import pallas as pl
from jax.experimental.pallas import tpu as pltpu
from jax.sharding import PartitionSpec as P

PB = 32
SWEEPS = 2


INV_FOUR_PI = 1.0 / (4.0 * math.pi)
CAP = 0.4
OMEGA = 1.5
EPS = 1e-06
LANES = 128
STEP = 256
BLOCK = 512
VMEM_BYTES = 58 << 20
FINISH_BYTES = 50 << 20
SMALL_BYTES = 4 << 20


def spread(block, axis, count):
    copies = jnp.broadcast_to(block[None], (count,) + block.shape)
    return lax.all_to_all(copies, axis, 0, 0, tiled=True)


def three(value):
    high = value.astype(jnp.bfloat16).astype(jnp.float32)
    rest = value - high
    middle = rest.astype(jnp.bfloat16).astype(jnp.float32)
    return high, middle, rest - middle


def factor_kernel(center_ref, normal_ref, area_ref, start_ref, factor_ref, shown_ref):
    @pl.when(pl.program_id(0) == 0)
    def _():
        shown = start_ref[...].astype(jnp.bfloat16)
        for device in range(shown_ref.shape[0]):
            shown_ref[device] = shown

    width = center_ref.shape[1]
    blank = jnp.zeros((4, width), jnp.float32)
    area = area_ref[...]
    place = jnp.concatenate([center_ref[...], area, blank], axis=0)
    scaled = normal_ref[...] * (area * INV_FOUR_PI)
    level = -jnp.sum(scaled * center_ref[...], axis=0, keepdims=True)
    high, middle, low = three(jnp.concatenate([scaled, level, blank], axis=0))
    at_level = lax.broadcasted_iota(jnp.int32, high.shape, 0) == 3
    bare = jnp.where(at_level, 0.0, high)
    bare_middle = jnp.where(at_level, 0.0, middle)
    none = jnp.zeros_like(high)
    rows = [high, bare, middle, bare, bare_middle, low, none, none]
    rows += list(three(place)) + [none] * 5
    factor_ref[...] = jnp.concatenate(rows, axis=0).T.astype(jnp.bfloat16)


def source_factors(centers, normals, areas, start, devices, block=1024):
    count = centers.shape[1]
    return pl.pallas_call(
        factor_kernel,
        grid=(count // block,),
        in_specs=[
            pl.BlockSpec((3, block), lambda i: (0, i)),
            pl.BlockSpec((3, block), lambda i: (0, i)),
            pl.BlockSpec((1, block), lambda i: (0, i)),
            pl.BlockSpec(start.shape, lambda i: (0, 0)),
        ],
        out_specs=[
            pl.BlockSpec((block, LANES), lambda i: (i, 0)),
            pl.BlockSpec((devices,) + start.shape, lambda i: (0, 0, 0)),
        ],
        out_shape=[
            jax.ShapeDtypeStruct((count, LANES), jnp.bfloat16),
            jax.ShapeDtypeStruct((devices,) + start.shape, jnp.bfloat16),
        ],
        cost_estimate=pl.CostEstimate(
            flops=count * 400, bytes_accessed=count * 400, transcendentals=0
        ),
        name="factors",
    )(centers, normals, areas[None, :], start)


def target_factors(targets):
    targets = jnp.concatenate([targets, jnp.zeros_like(targets)], axis=0)
    high = targets.astype(jnp.bfloat16).astype(jnp.float32)
    rest = targets - high
    middle = rest.astype(jnp.bfloat16).astype(jnp.float32)
    low = rest - middle
    rows = [high, middle, high, low, middle, high]
    return jnp.concatenate(rows, axis=0).astype(jnp.bfloat16)


def fill(factor_ref, target_ref, wide_ref, pair_ref, column, stores):
    facing = jnp.dot(
        factor_ref[:, :48],
        pair_ref[:, column : column + STEP],
        preferred_element_type=jnp.float32,
    )
    for lane in range(0, STEP, LANES):
        here = slice(column + lane, column + lane + LANES)
        x, y, z = (target_ref[d : d + 1, here] for d in range(3))
        for row in range(0, BLOCK, 16):
            at = slice(row, row + 16)
            delta_x = x - wide_ref[0, at, :]
            delta_y = y - wide_ref[1, at, :]
            delta_z = z - wide_ref[2, at, :]
            dist_sq = delta_x * delta_x + delta_y * delta_y + delta_z * delta_z + wide_ref[3, at, :]
            inverse = lax.rsqrt(dist_sq)
            value = facing[row : row + 16, lane : lane + LANES] * (inverse * inverse * inverse)
            value = value.astype(jnp.bfloat16)
            for store in stores:
                store[at, here] = value


def prepare(target_ref, pair_ref, spread_ref):
    pair_ref[...] = target_factors(target_ref[...])
    which = lax.broadcasted_iota(jnp.int32, spread_ref.shape, 0)
    lane = lax.broadcasted_iota(jnp.int32, spread_ref.shape, 1)
    chosen = which % 8 == lane // LANES
    spread_ref[...] = jnp.where(chosen, 1.0, 0.0).astype(jnp.bfloat16)


def spread_params(factor_ref, spread_ref, wide_ref):
    wide = jnp.dot(factor_ref[:, 64:96], spread_ref[...], preferred_element_type=jnp.float32)
    for row in range(4):
        wide_ref[row] = wide[:, row * LANES : (row + 1) * LANES]


def build_kernel(factor_ref, target_ref, tile_ref, wide_ref, pair_ref, spread_ref):
    @pl.when(pl.program_id(0) == 0)
    def _():
        prepare(target_ref, pair_ref, spread_ref)

    spread_params(factor_ref, spread_ref, wide_ref)
    for column in range(0, tile_ref.shape[1], STEP):
        fill(factor_ref, target_ref, wide_ref, pair_ref, column, [tile_ref])


def finish_kernel(
    factor_ref,
    target_ref,
    moved_ref,
    old_ref,
    tile_ref,
    product_ref,
    wide_ref,
    pair_ref,
    spread_ref,
    even_ref,
    odd_ref,
):
    step = pl.program_id(0)
    blocks = pl.num_programs(0) - 1
    width = tile_ref.shape[1]
    deep = BLOCK // LANES

    @pl.when(step == 0)
    def _():
        prepare(target_ref, pair_ref, spread_ref)
        product_ref[...] = jnp.zeros_like(product_ref)

    def dot(block, ref, column):
        part = jnp.concatenate([moved_ref[deep * block + i] for i in range(deep)], axis=1)
        return jnp.dot(
            part, ref[:, column : column + STEP], preferred_element_type=jnp.float32
        )

    def add_to(column, value):
        for lane in range(0, STEP, LANES):
            product_ref[(column + lane) // LANES] += value[:, lane : lane + LANES]

    def whole(now_ref, before_ref):
        spread_params(factor_ref, spread_ref, wide_ref)
        for column in range(0, width, STEP):
            value = dot(step, old_ref, column)
            if before_ref is not None:
                value += dot(blocks + step - 1, before_ref, column)
            fill(
                factor_ref, target_ref, wide_ref, pair_ref, column, [tile_ref, now_ref]
            )
            add_to(column, value)

    @pl.when(step == 0)
    def _():
        whole(even_ref, None)

    @pl.when((step > 0) & (step < blocks) & (step % 2 == 0))
    def _():
        whole(even_ref, odd_ref)

    @pl.when((step < blocks) & (step % 2 == 1))
    def _():
        whole(odd_ref, even_ref)

    @pl.when((step == blocks) & (step % 2 == 0))
    def _():
        for column in range(0, width, STEP):
            add_to(column, dot(blocks + step - 1, odd_ref, column))

    @pl.when((step == blocks) & (step % 2 == 1))
    def _():
        for column in range(0, width, STEP):
            add_to(column, dot(blocks + step - 1, even_ref, column))


def build(factors, targets):
    count = factors.shape[0]
    width = targets.shape[1]
    return pl.pallas_call(
        build_kernel,
        grid=(count // BLOCK // 2,),
        in_specs=[
            pl.BlockSpec((BLOCK, LANES), lambda i: (i, 0)),
            pl.BlockSpec((4, width), lambda i: (0, 0)),
        ],
        out_specs=pl.BlockSpec((BLOCK, width), lambda i: (i, 0)),
        out_shape=pltpu.HBM((count, width), jnp.bfloat16),
        scratch_shapes=[
            pltpu.VMEM((4, BLOCK, LANES), jnp.float32),
            pltpu.VMEM((48, width), jnp.bfloat16),
            pltpu.VMEM((32, 4 * LANES), jnp.bfloat16),
        ],
        compiler_params=pltpu.CompilerParams(vmem_limit_bytes=VMEM_BYTES),
        cost_estimate=pl.CostEstimate(
            flops=count * width * 50, bytes_accessed=count * width, transcendentals=count * width // 2
        ),
        name="build",
    )(factors, targets)


def finish_build(factors, targets, moved, tile):
    count, width = tile.shape
    blocks = count // BLOCK // 2
    onsets = moved.shape[1]
    return pl.pallas_call(
        finish_kernel,
        grid=(blocks + 1,),
        in_specs=[
            pl.BlockSpec((BLOCK, LANES), lambda i: (blocks + jnp.minimum(i, blocks - 1), 0)),
            pl.BlockSpec((4, width), lambda i: (0, 0)),
            pl.BlockSpec(moved.shape, lambda i: (0, 0, 0)),
            pl.BlockSpec((BLOCK, width), lambda i: (jnp.minimum(i, blocks - 1), 0)),
        ],
        out_specs=[
            pl.BlockSpec((BLOCK, width), lambda i: (blocks + jnp.minimum(i, blocks - 1), 0)),
            pl.BlockSpec((width // LANES, onsets, LANES), lambda i: (0, 0, 0)),
        ],
        out_shape=[
            pltpu.HBM((count, width), jnp.bfloat16),
            jax.ShapeDtypeStruct((width // LANES, onsets, LANES), jnp.float32),
        ],
        scratch_shapes=[
            pltpu.VMEM((4, BLOCK, LANES), jnp.float32),
            pltpu.VMEM((48, width), jnp.bfloat16),
            pltpu.VMEM((32, 4 * LANES), jnp.bfloat16),
            pltpu.VMEM((BLOCK, width), jnp.bfloat16),
            pltpu.VMEM((BLOCK, width), jnp.bfloat16),
        ],
        input_output_aliases={3: 0},
        compiler_params=pltpu.CompilerParams(vmem_limit_bytes=FINISH_BYTES),
        name="finish",
    )(factors, targets, moved, tile)


def apply_kernel(moved_ref, tile_ref, product_ref):
    step = pl.program_id(0)
    chunks = range(tile_ref.shape[1] // LANES)
    part = jnp.concatenate([moved_ref[i] for i in range(moved_ref.shape[0])], axis=1)
    product = jnp.dot(part, tile_ref[...], preferred_element_type=jnp.float32)

    @pl.when(step == 0)
    def _():
        for chunk in chunks:
            product_ref[chunk] = product[:, chunk * LANES : (chunk + 1) * LANES]

    @pl.when(step > 0)
    def _():
        for chunk in chunks:
            product_ref[chunk] += product[:, chunk * LANES : (chunk + 1) * LANES]


def apply(moved, tile, depth=2048):
    count, width = tile.shape
    onsets = moved.shape[1]
    return pl.pallas_call(
        apply_kernel,
        grid=(count // depth,),
        in_specs=[
            pl.BlockSpec((depth // LANES, onsets, LANES), lambda i: (i, 0, 0)),
            pl.BlockSpec((depth, width), lambda i: (i, 0)),
        ],
        out_specs=pl.BlockSpec((width // LANES, onsets, LANES), lambda i: (0, 0, 0)),
        out_shape=jax.ShapeDtypeStruct((width // LANES, onsets, LANES), jnp.float32),
        compiler_params=pltpu.CompilerParams(vmem_limit_bytes=VMEM_BYTES),
        name="apply",
    )(moved, tile)


def residual_kernel(part_ref, base_ref, residual_ref, sent_ref):
    residual = base_ref[...] - jnp.sum(part_ref[...], axis=0)
    residual_ref[...] = residual
    sent = residual.astype(jnp.bfloat16)
    for device in range(sent_ref.shape[0]):
        sent_ref[device] = sent


def residual_of(parts, base, devices):
    return pl.pallas_call(
        residual_kernel,
        in_specs=[WHOLE] * 2,
        out_specs=[WHOLE] * 2,
        out_shape=[
            jax.ShapeDtypeStruct(base.shape, jnp.float32),
            jax.ShapeDtypeStruct((devices,) + base.shape, jnp.bfloat16),
        ],
        compiler_params=pltpu.CompilerParams(vmem_limit_bytes=SMALL_BYTES),
        name="residual",
    )(parts, base)


def sums_kernel(part_ref, start_ref, residual_ref, center_ref, area_ref, field_ref, sent_ref):
    change = jnp.sum(part_ref[...], axis=0)
    residual = residual_ref[...]
    count = residual.shape[0]
    field_ref[:count] = start_ref[...]
    field_ref[count : 2 * count] = residual
    field_ref[2 * count : 3 * count] = change
    field_ref[3 * count :] = center_ref[...]
    area = jnp.broadcast_to(area_ref[...], residual.shape)
    weighted = area * residual
    terms = [weighted * residual, weighted * change, area * change * change, area]
    total = jnp.sum(jnp.concatenate(terms, axis=0).T, axis=0, keepdims=True)
    for device in range(sent_ref.shape[0]):
        sent_ref[device] = jnp.broadcast_to(total, sent_ref.shape[1:])


def sums_of(parts, start, residual, centers, areas, devices):
    count, own = start.shape
    return pl.pallas_call(
        sums_kernel,
        in_specs=[WHOLE] * 5,
        out_specs=[WHOLE] * 2,
        out_shape=[
            jax.ShapeDtypeStruct((3 * count + 8, own), jnp.float32),
            jax.ShapeDtypeStruct((devices, 2, 4 * count), jnp.float32),
        ],
        compiler_params=pltpu.CompilerParams(vmem_limit_bytes=SMALL_BYTES),
        name="sums",
    )(parts, start, residual, centers, areas)


def regroup_kernel(part_ref, sent_ref):
    sent = jnp.broadcast_to(jnp.sum(part_ref[...], axis=0)[0:1, :], sent_ref.shape[1:])
    for device in range(sent_ref.shape[0]):
        sent_ref[device] = sent


def regroup(parts, devices):
    return pl.pallas_call(
        regroup_kernel,
        in_specs=[WHOLE],
        out_specs=WHOLE,
        out_shape=jax.ShapeDtypeStruct((devices, 8, parts.shape[2]), jnp.float32),
        compiler_params=pltpu.CompilerParams(vmem_limit_bytes=SMALL_BYTES),
        name="regroup",
    )(parts)


def last_kernel(
    part_ref, field_ref, before_ref, after_ref, onset_ref, end_ref, state_ref, pressure_ref
):
    count, own = state_ref.shape
    total = jnp.sum(part_ref[...], axis=0)[0:1, :]
    total = jnp.broadcast_to(total, (4 * count, own)).T
    both, mixed, changed, area = (total[i * count : (i + 1) * count] for i in range(4))
    reach = CAP * jnp.sqrt(area)

    def damp(sums):
        return OMEGA * jnp.minimum(1.0, reach * lax.rsqrt(sums + EPS))

    one = damp(both)
    keep = 1.0 - 0.5 * one
    sums = keep * keep * both - 2.0 * keep * one * mixed + one * one * changed
    two = damp(jnp.maximum(sums, 0.0))
    on_residual = one + two * keep
    on_change = two * one

    def strengths(ref):
        value = ref[:count] + on_residual * ref[count : 2 * count]
        return value - on_change * ref[2 * count : 3 * count]

    state = strengths(field_ref)
    state_ref[...] = state

    def differences(middle, low, high):
        lane = lax.broadcasted_iota(jnp.int32, middle.shape, 1)
        is_first = jnp.broadcast_to(end_ref[0], middle.shape) == 1
        is_last = jnp.broadcast_to(end_ref[1], middle.shape) == 1
        low = jnp.where(is_first, middle, pltpu.roll(low, PB, 1))
        high = jnp.where(is_last, middle, pltpu.roll(high, own - PB, 1))
        lower = jnp.where(lane < PB, low, pltpu.roll(middle, PB, 1))
        upper = jnp.where(lane >= own - PB, high, pltpu.roll(middle, own - PB, 1))
        around = lane % PB
        following = jnp.where(
            around == PB - 1, pltpu.roll(middle, PB - 1, 1), pltpu.roll(middle, own - 1, 1)
        )
        preceding = jnp.where(
            around == 0, pltpu.roll(middle, own - PB + 1, 1), pltpu.roll(middle, 1, 1)
        )
        return upper - lower, following - preceding

    steps = differences(field_ref[3 * count :], before_ref[3 * count :], after_ref[3 * count :])
    changes = differences(state, strengths(before_ref), strengths(after_ref))
    pressure = jnp.ones_like(state)
    for step, change in zip(steps, changes):
        span = jnp.sqrt(jnp.sum(step * step, axis=0, keepdims=True))
        along = onset_ref[:, 0:1] * step[0:1]
        along += onset_ref[:, 1:2] * step[1:2]
        along += onset_ref[:, 2:3] * step[2:3]
        speed = along / span - change / span
        pressure -= speed * speed
    pressure_ref[...] = pressure


def last(parts, fields, before, after, onset, ends, count):
    own = fields.shape[1]
    return pl.pallas_call(
        last_kernel,
        in_specs=[WHOLE] * 5 + [pl.BlockSpec(memory_space=pltpu.SMEM)],
        out_specs=[WHOLE] * 2,
        out_shape=[jax.ShapeDtypeStruct((count, own), jnp.float32)] * 2,
        compiler_params=pltpu.CompilerParams(vmem_limit_bytes=SMALL_BYTES),
        name="last",
    )(parts, fields, before, after, onset, ends)


WHOLE = pl.BlockSpec(memory_space=pltpu.VMEM)


def per_device(centers, normals, areas, onset, start):
    row_count = lax.axis_size("row")
    col_count = lax.axis_size("col")
    row_index = lax.axis_index("row")
    col_index = lax.axis_index("col")
    own = start.shape[1]
    count = start.shape[0]
    own_first = col_index * own
    own_areas = lax.dynamic_slice_in_dim(areas, own_first, own, 0)
    own_normals = lax.dynamic_slice_in_dim(normals, own_first, own, 1)
    own_centers = lax.dynamic_slice_in_dim(centers, own_first, own, 1)

    note = jnp.concatenate([own_centers, jnp.ones((1, own), jnp.float32)], axis=0)
    notes = spread(note, "row", row_count)
    factors, shown = source_factors(centers, normals, areas, start, col_count)
    right = -jnp.sum(onset[:, :, None] * own_normals[:, None, :], axis=0)
    base = right - 0.5 * start
    notes, shown, factors, base = lax.optimization_barrier((notes, shown, factors, base))
    targets = jnp.transpose(notes, (1, 0, 2)).reshape(4, row_count * own)
    moved = lax.all_to_all(shown, "col", 0, 0, tiled=True)

    targets = pltpu.with_memory_space_constraint(targets, pltpu.HBM)
    tile = build(factors, targets)
    tile, partial = finish_build(factors, targets, moved, tile)

    parts = lax.all_to_all(partial, "row", 0, 0, tiled=True)
    residual, sent = residual_of(parts, base, col_count)
    gathered = lax.all_to_all(sent, "col", 0, 0, tiled=True)
    partial = apply(gathered, tile)
    parts = lax.all_to_all(partial, "row", 0, 0, tiled=True)
    here = jnp.pad(own_centers, ((0, 5), (0, 0)))
    fields, sent = sums_of(parts, start, residual, here, own_areas[None, :], col_count)

    flat = row_index * col_count + col_index
    devices = row_count * col_count
    forward = [(i, i + 1) for i in range(devices - 1)]
    backward = [(i + 1, i) for i in range(devices - 1)]
    parts = lax.all_to_all(sent, "col", 0, 0, tiled=True)
    before = lax.ppermute(fields, ("row", "col"), forward)
    sent, before, later = lax.optimization_barrier((regroup(parts, row_count), before, fields))
    after = lax.ppermute(later, ("row", "col"), backward)
    parts = lax.all_to_all(sent, "row", 0, 0, tiled=True)
    ends = jnp.stack([flat == 0, flat == devices - 1]).astype(jnp.int32)
    return last(parts, fields, before, after, onset.T, ends, count)


def solution(mesh):
    return jax.shard_map(
        per_device,
        mesh=mesh,
        in_specs=(P(None, "row"), P(None, "row"), P("row"), P(), P(None, ("row", "col"))),
        out_specs=(P(None, ("row", "col")), P(None, ("row", "col"))),
        check_vma=False,
    )
```
